32 devices in a mesh: fsdp: 4 (over y, core), ctx: 4 (over z), uly: 2 (over x).
Axes of the slice: x: 2, y: 2, z: 4, core: 2. Of those that a mesh axis runs over, the one named last changes fastest.
Arguments:
- query_states: bfloat16 [12, 384, 8192], P('fsdp', 'ctx', 'uly'), may hold values from -8 to 8
- key_projections: bfloat16 [12, 384, 1024], P('fsdp', 'ctx', 'uly'), may hold values from -8 to 8
- value_projections: bfloat16 [12, 384, 1024], P('fsdp', 'ctx', 'uly'), may hold values from -6 to 6
- layer_bias: bfloat16 [10240], P('fsdp'), may hold values from -3 to 3
- positions: int32 [12, 384], P('fsdp', 'ctx'), may hold values from 0 to 383, as said below
- rescale: float32 [2, 64], replicated, may hold values from 1 to 16
- table_index: int32 [12], P('fsdp'), may hold values from 0 to 1
Outputs:
- attended: bfloat16 [12, 384, 8192], P('fsdp', 'ctx', 'uly')
The draws below stay inside these ranges and needn't reach their ends.
Inputs may be any that keep to these rules, and one draw needn't show every extreme that they name: In each sequence the rows come in aligned runs of 48; every run holds 48 consecutive positions in increasing order, starting at a multiple of 48, and every position 0 to 383 occurs once. The order of the runs differs between sequences.
All inputs are finite; a program needn't handle non-finite values.
Results may differ from the reference program's by a relative error of at most 0.012.
Values may be sent and summed in bfloat16 or wider, within the bound.
A program may use at most 64 MiB of HBM per device.

```python
import math
import jax
import jax.numpy as jnp
from jax import lax

QUERY_HEADS = 64
KEY_VALUE_HEADS = 8
HEAD_SIZE = 128
TABLES = 2
SEQUENCE_ROWS = 384
BATCH_COUNT = 12
BLOCK = 48
BIAS_LEN = 10240


def draw_query_states(key, part):
    noise_key = jax.random.fold_in(key, 17)
    complete_shape = (BATCH_COUNT, SEQUENCE_ROWS, QUERY_HEADS, HEAD_SIZE)
    value_entries = jnp.clip(2.0 * jax.random.normal(noise_key, complete_shape, jnp.float32), -8.0, 8.0)
    return value_entries.reshape(BATCH_COUNT, SEQUENCE_ROWS, QUERY_HEADS * HEAD_SIZE).astype(jnp.bfloat16)


def draw_key_projections(key, part):
    noise_key = jax.random.fold_in(key, 23)
    complete_shape = (BATCH_COUNT, SEQUENCE_ROWS, KEY_VALUE_HEADS, HEAD_SIZE)
    value_entries = jnp.clip(jax.random.normal(noise_key, complete_shape, jnp.float32), -8.0, 8.0)
    return value_entries.reshape(BATCH_COUNT, SEQUENCE_ROWS, KEY_VALUE_HEADS * HEAD_SIZE).astype(jnp.bfloat16)


def order_of(branch_key):
    return jax.random.permutation(branch_key, SEQUENCE_ROWS // BLOCK)


def draw_positions(key, part):
    orders = jax.vmap(order_of)(jax.random.split(key, BATCH_COUNT))
    row_index = jnp.arange(SEQUENCE_ROWS)
    return (orders[:, row_index // BLOCK] * BLOCK + row_index % BLOCK).astype(jnp.int32)


def touch_ends(result, own_key, smallest, top_value):
    longest = result.shape.index(max(result.shape))
    spots = []
    for shift in (0, 1):
        where = [jax.random.randint(jax.random.fold_in(own_key, axis), (), 0, length) for axis, length in enumerate(result.shape)]
        where[longest] = (where[longest] + shift) % result.shape[longest]
        spots.append(tuple(where))
    return result.at[spots[0]].set(smallest).at[spots[1]].set(top_value)


def levels(rng, dims, shards, smallest, largest):
    def one(axis_at, blocks):
        draws = jax.random.uniform(jax.random.fold_in(jax.random.fold_in(rng, 6), axis_at), (blocks,), jnp.float32, smallest / len(shards), largest / len(shards))
        return jnp.repeat(jnp.exp(draws), dims[axis_at] // blocks).reshape((-1,) + (1,) * (len(dims) - axis_at - 1))

    level = one(*shards[0])
    for cut in shards[1:]:
        level = level * one(*cut)
    return level


def gaussian(stream_key, dims, width, limit, cuts=(), kind=jnp.bfloat16):
    factor_of = levels(stream_key, dims, cuts, -0.22, 0.18) if cuts else 1.0
    result = jax.random.normal(stream_key, dims, jnp.float32) * width * factor_of
    return jnp.minimum(jnp.maximum(result, -limit), limit).astype(kind)


def setup_inputs(seed: int = 0) -> dict:
    keys = jax.random.split(jax.random.key(seed), 8)
    return {
        "query_states": draw_query_states(jax.random.fold_in(keys[7], 71), 0),
        "key_projections": draw_key_projections(jax.random.fold_in(keys[7], 71), 0),
        "value_projections": gaussian(keys[2], (BATCH_COUNT, SEQUENCE_ROWS, KEY_VALUE_HEADS * HEAD_SIZE), 1.0, 6.0, ((0, 4), (1, 4), (2, 2))),
        "layer_bias": gaussian(keys[3], (BIAS_LEN,), 0.5, 3.0, ((0, 4),)),
        "positions": draw_positions(jax.random.fold_in(keys[7], 71), 0),
        "rescale": jnp.clip(jnp.exp(jax.random.uniform(keys[5], (TABLES, HEAD_SIZE // 2), jnp.float32, math.log(1.0), math.log(16.0))), 1.0, 16.0),
        "table_index": touch_ends(jax.random.randint(keys[6], (BATCH_COUNT,), 0, TABLES), jax.random.fold_in(keys[6], 1), 0, TABLES - 1).astype(jnp.int32),
    }


rope_base = 1000000.0
masked_value = -1e+30

def apply_rotation(states, positions, scale_factors):
    half_dim = states.shape[-1] // 2
    exponent = jnp.arange(half_dim, dtype=jnp.float32) * (2.0 / states.shape[-1])
    inverse = 1.0 / (scale_factors * jnp.power(jnp.float32(rope_base), exponent)[None, :])
    angles = positions.astype(jnp.float32)[:, :, None] * inverse[:, None, :]
    cosine = jnp.cos(angles)[:, :, None, :]
    sine_wave = jnp.sin(angles)[:, :, None, :]
    leading = states[..., :half_dim]
    trailing = states[..., half_dim:]
    return jnp.concatenate([leading * cosine - trailing * sine_wave, trailing * cosine + leading * sine_wave], axis=-1)

def attend_group(operands):
    query_rows, key_rows, value_rows, row_positions = operands
    scores = jnp.einsum('qrd,kd->rqk', query_rows.astype(jnp.float32), key_rows.astype(jnp.float32)) / math.sqrt(HEAD_SIZE)
    allowed = row_positions[None, :] <= row_positions[:, None]
    highest = lax.optimization_barrier(jnp.max(jnp.where(allowed[None], scores, masked_value), axis=-1, keepdims=True))
    weights = jnp.where(allowed[None], jnp.exp(scores - highest), 0.0)
    totals = lax.optimization_barrier(jnp.sum(weights, axis=-1))
    rounded = lax.optimization_barrier(weights.astype(jnp.bfloat16))
    weighted_blend = jnp.einsum('rqk,kd->qrd', rounded.astype(jnp.float32), value_rows.astype(jnp.float32))
    return weighted_blend / jnp.transpose(totals)[:, :, None]

def reference(query_states, key_projections, value_projections, layer_bias, positions, rescale, table_index):
    bias_terms = layer_bias.astype(jnp.float32)
    query_span_width = QUERY_HEADS * HEAD_SIZE
    key_span_width = KEY_VALUE_HEADS * HEAD_SIZE
    query_bias = bias_terms[:query_span_width].reshape(QUERY_HEADS, HEAD_SIZE)
    key_offset_bias = bias_terms[query_span_width:query_span_width + key_span_width].reshape(KEY_VALUE_HEADS, HEAD_SIZE)
    value_offset_bias = bias_terms[query_span_width + key_span_width:].reshape(KEY_VALUE_HEADS, HEAD_SIZE)
    scale_factors = rescale[table_index]
    query_rotated_rows = apply_rotation(query_states.astype(jnp.float32).reshape(BATCH_COUNT, SEQUENCE_ROWS, QUERY_HEADS, HEAD_SIZE) + query_bias, positions, scale_factors).astype(jnp.bfloat16)
    key_rotated_rows = apply_rotation(key_projections.astype(jnp.float32).reshape(BATCH_COUNT, SEQUENCE_ROWS, KEY_VALUE_HEADS, HEAD_SIZE) + key_offset_bias, positions, scale_factors).astype(jnp.bfloat16)
    value_with_bias = (value_projections.astype(jnp.float32).reshape(BATCH_COUNT, SEQUENCE_ROWS, KEY_VALUE_HEADS, HEAD_SIZE) + value_offset_bias).astype(jnp.bfloat16)
    group_fraction = QUERY_HEADS // KEY_VALUE_HEADS
    grouped_rows = query_rotated_rows.reshape(BATCH_COUNT, SEQUENCE_ROWS, KEY_VALUE_HEADS, group_fraction, HEAD_SIZE).transpose(0, 2, 1, 3, 4).reshape(BATCH_COUNT * KEY_VALUE_HEADS, SEQUENCE_ROWS, group_fraction, HEAD_SIZE)
    key_group_rows = key_rotated_rows.transpose(0, 2, 1, 3).reshape(BATCH_COUNT * KEY_VALUE_HEADS, SEQUENCE_ROWS, HEAD_SIZE)
    value_group_rows = value_with_bias.transpose(0, 2, 1, 3).reshape(BATCH_COUNT * KEY_VALUE_HEADS, SEQUENCE_ROWS, HEAD_SIZE)
    position_group_rows = jnp.broadcast_to(positions[:, None, :], (BATCH_COUNT, KEY_VALUE_HEADS, SEQUENCE_ROWS)).reshape(BATCH_COUNT * KEY_VALUE_HEADS, SEQUENCE_ROWS)
    weighted_blend = lax.map(attend_group, (grouped_rows, key_group_rows, value_group_rows, position_group_rows))
    output_rows = weighted_blend.reshape(BATCH_COUNT, KEY_VALUE_HEADS, SEQUENCE_ROWS, group_fraction, HEAD_SIZE).transpose(0, 2, 1, 3, 4).reshape(BATCH_COUNT, SEQUENCE_ROWS, QUERY_HEADS * HEAD_SIZE)
    return output_rows.astype(jnp.bfloat16)
```

```python
import functools
import math

import jax
import jax.numpy as jnp
from jax import lax
from jax.experimental import pallas as pl
from jax.experimental.pallas import tpu as pltpu
from jax.sharding import PartitionSpec as P

QUERY_HEADS = 64
KEY_VALUE_HEADS = 8
HEAD_SIZE = 128
GROUP = QUERY_HEADS // KEY_VALUE_HEADS
RUN = 48

rope_base = 1000000.0
masked_value = -1e30
MESH = pl.DeviceIdType.MESH


def sine_cosine(angle):
    turns = jnp.floor(angle * (2.0 / math.pi) + 0.5)
    r = angle - turns * 1.5703125
    r = r - turns * 4.837512969970703125e-4
    r = r - turns * 7.54978995489188216e-8
    z = r * r
    s = r + r * z * (-1.6666654611e-1 + z * (8.3321608736e-3 - z * 1.9515295891e-4))
    c = 1.0 - 0.5 * z + z * z * (
        4.166664568298827e-2 + z * (-1.388731625493765e-3 + z * 2.443315711809948e-5)
    )
    quarter = turns.astype(jnp.int32) & 3
    odd = (quarter & 1) == 1
    sine = jnp.where(odd, c, s)
    cosine = jnp.where(odd, s, c)
    sine = jnp.where(quarter >= 2, -sine, sine)
    cosine = jnp.where((quarter == 1) | (quarter == 2), -cosine, cosine)
    return sine, cosine


def chunk_list(batch, heads_kv):
    chunks = [(b, 0, heads_kv) for b in range(batch - 1)]
    return chunks + [(batch - 1, g, 1) for g in range(heads_kv)]


def kernel(
    n, nf, heads_at_once,
    table_hbm, q_hbm, k_hbm, v_hbm, bias_hbm, pos_hbm, rescale_hbm,
    out_ref,
    table_ref, pos_buf, rescale_ref, small_sem,
    q_buf, q_rot, k_buf, v_buf, cos_t, sin_t, mask_near, mask_far, bias_buf, bias_f,
    acc, high_buf, total_buf,
    q_sem, own_sem, send_right, send_left, recv_sem,
    pos_send, pos_recv, bias_send, bias_recv, spread_send, spread_recv, ready,
):
    batch, rows, _ = q_hbm.shape
    heads_kv = k_hbm.shape[2] // HEAD_SIZE
    units = batch * heads_kv
    me = lax.axis_index("ctx")
    mf = lax.axis_index("fsdp")
    mu = lax.axis_index("uly")
    shard_rows = bias_hbm.shape[0]
    chunks = chunk_list(batch, heads_kv)
    wide = GROUP * HEAD_SIZE
    off = jnp.where(2 * me <= n - 1, 0, 1)
    far = jnp.where(2 * me <= n - 1, n - 1, 0)

    barrier = pltpu.get_barrier_semaphore()

    @pl.when(me > 0)
    def _():
        pl.semaphore_wait(barrier, 1)

    @pl.when(me < n - 1)
    def _():
        pl.semaphore_signal(barrier, inc=1, device_id={"ctx": me + 1}, device_id_type=MESH)

    @pl.when(me == 0)
    def _():
        for d in range(1, nf):
            pl.semaphore_signal(
                barrier, inc=1, device_id={"fsdp": lax.rem(mf + d, nf)}, device_id_type=MESH
            )
        pl.semaphore_wait(barrier, nf - 1)

    def pos_copy(source, target):
        return pltpu.make_async_remote_copy(
            src_ref=pos_hbm, dst_ref=pos_buf.at[source],
            send_sem=pos_send.at[target], recv_sem=pos_recv.at[source],
            device_id={"ctx": target}, device_id_type=MESH,
        )

    def parts(c):
        b, g, count = chunks[c]
        return b, slice(None), pl.ds(g * HEAD_SIZE, count * HEAD_SIZE)

    def remote(shard, c, own, sems, target):
        at = parts(c)
        return [
            pltpu.make_async_remote_copy(
                src_ref=hbm.at[at] if own else buf.at[(shard,) + at],
                dst_ref=buf.at[(shard,) + at],
                send_sem=sems.at[shard, c, i], recv_sem=recv_sem.at[shard, c, i],
                device_id={"ctx": target}, device_id_type=MESH,
            )
            for i, (hbm, buf) in enumerate(((k_hbm, k_buf), (v_hbm, v_buf)))
        ]

    def to_right(shard, c, own=False):
        return remote(shard, c, own, send_right, lax.rem(me + 1, n))

    def to_left(shard, c, own=False):
        return remote(shard, c, own, send_left, lax.rem(me + n - 1, n))

    def send_left_own():
        for c in range(len(chunks)):
            for copy in to_left(me, c, True):
                copy.start()

    @pl.when(me > 0)
    def _():
        for j in range(n - 1):
            @pl.when(j < me)
            def _():
                pos_copy(me, j).start()

    @pl.when((me > 0) & (mf % 2 == 0))
    def _():
        send_left_own()

    for j in range(n - 1):
        @pl.when(j < me)
        def _():
            pl.semaphore_signal(
                ready.at[me], inc=1, device_id={"ctx": j}, device_id_type=MESH
            )

    small = [
        pltpu.make_async_copy(source, target, small_sem.at[i])
        for i, (source, target) in enumerate(
            (
                (pos_hbm, pos_buf.at[me]), (rescale_hbm, rescale_ref),
                (table_hbm, table_ref),
            )
        )
    ]
    own_bias = pltpu.make_async_copy(bias_hbm, bias_buf.at[mf], small_sem.at[3])
    for copy in small:
        copy.start()

    @pl.when(me == 0)
    def _():
        own_bias.start()

    def q_copy(b):
        return pltpu.make_async_copy(q_hbm.at[b], q_buf.at[b], q_sem.at[b])

    def own_copies(b):
        return (
            pltpu.make_async_copy(k_hbm.at[b], k_buf.at[me, b], own_sem.at[b, 0]),
            pltpu.make_async_copy(v_hbm.at[b], v_buf.at[me, b], own_sem.at[b, 1]),
        )

    for b in range(batch):
        q_copy(b).start()
    for b in range(batch):
        for copy in own_copies(b):
            copy.start()
    for copy in small:
        copy.wait()

    @pl.when((me > 0) & (mf % 2 == 1))
    def _():
        send_left_own()

    def bias_copy(source, target):
        return pltpu.make_async_remote_copy(
            src_ref=bias_hbm, dst_ref=bias_buf.at[source],
            send_sem=bias_send.at[target], recv_sem=bias_recv.at[source],
            device_id={"fsdp": target}, device_id_type=MESH,
        )

    def spread_copy(target):
        return pltpu.make_async_remote_copy(
            src_ref=bias_buf, dst_ref=bias_buf,
            send_sem=spread_send.at[target], recv_sem=spread_recv,
            device_id={"ctx": target}, device_id_type=MESH,
        )

    @pl.when(me == 0)
    def _():
        for d in range(1, nf):
            bias_copy(mf, lax.rem(mf + d, nf)).start()
        own_bias.wait()
        for d in range(1, nf):
            other = lax.rem(mf + d, nf)
            bias_copy(other, other).wait_recv()

    for j in range(1, n):
        @pl.when(me < j)
        def _():
            pl.semaphore_wait(ready.at[j], 1)
            pos_copy(me, j).start()

        @pl.when((me < j) & (me == 0))
        def _():
            spread_copy(j).start()

    @pl.when(me < n - 1)
    def _():
        for c in range(len(chunks)):
            for copy in to_right(me, c, True):
                copy.start()

    @pl.when(me > 0)
    def _():
        spread_copy(0).wait_recv()

    for f in range(nf):
        bias_f[f] = bias_buf[f].astype(jnp.float32)

    def bias_row(row):
        return bias_f[row // shard_rows, pl.ds(row % shard_rows, 1), :]

    for j in range(n):
        @pl.when(j != me)
        def _():
            pos_copy(j, j).wait_recv()

    lane = lax.broadcasted_iota(jnp.int32, (1, HEAD_SIZE), 1)
    power = jnp.exp(
        (lane % (HEAD_SIZE // 2)).astype(jnp.float32)
        * (2.0 / HEAD_SIZE * math.log(rope_base))
    )
    low_half = lane < HEAD_SIZE // 2
    run_rows = lax.broadcasted_iota(jnp.int32, (RUN, HEAD_SIZE), 0)
    query_row = lax.broadcasted_iota(jnp.int32, (RUN, 1), 0)

    def masks(b, target, shards):
        key_lane = lax.broadcasted_iota(jnp.int32, (1, len(shards) * rows), 1)
        key_pos = key_lane % RUN
        for k, j in enumerate(shards):
            for piece in range(rows // RUN):
                first = pos_buf[j, b : b + 1, piece * RUN : piece * RUN + 1]
                here = key_lane // RUN == k * (rows // RUN) + piece
                key_pos = key_pos + jnp.where(here, first, 0)
        for piece in range(rows // RUN):
            first = pos_buf[me, b : b + 1, piece * RUN : piece * RUN + 1]
            allowed = key_pos <= query_row + first
            target[b, piece * RUN : (piece + 1) * RUN, :] = jnp.where(
                allowed, 0.0, masked_value
            )

    for b in range(batch):
        factors = rescale_ref[0:1, :]
        for t in range(1, rescale_ref.shape[0]):
            factors = jnp.where(table_ref[b] == t, rescale_ref[t : t + 1, :], factors)
        inverse = 1.0 / (jnp.concatenate([factors, factors], axis=1) * power)
        for j in range(n):
            for piece in range(rows // RUN):
                first = pos_buf[j, b : b + 1, piece * RUN : piece * RUN + 1]
                place = (run_rows + first).astype(jnp.float32)
                sine, cosine = sine_cosine(place * inverse)
                block = slice(piece * RUN, (piece + 1) * RUN)
                cos_t[b, j, block, :] = cosine
                sin_t[b, j, block, :] = jnp.where(low_half, -sine, sine)
        masks(b, mask_near, [off + k for k in range(n - 1)])
        masks(b, mask_far, [far])

    def rotate(x, cosine, sine):
        return x * cosine + pltpu.roll(x, HEAD_SIZE // 2, 1) * sine

    query_heads_here = heads_kv * GROUP
    for b in range(batch):
        q_copy(b).wait()

        @pl.loop(0, heads_kv)
        def _(g):
            for i in range(GROUP):
                x = q_buf[
                    b, :, pl.ds(pl.multiple_of(g * wide + i * HEAD_SIZE, HEAD_SIZE), HEAD_SIZE)
                ].astype(jnp.float32)
                x = x + bias_row(mu * query_heads_here + g * GROUP + i)
                q_rot[b * heads_kv + g, i * rows : (i + 1) * rows, :] = rotate(
                    x, cos_t[b, me], sin_t[b, me]
                ).astype(jnp.bfloat16)

    for b in range(batch):
        for copy in own_copies(b):
            copy.wait()

    scale = math.log2(math.e) / math.sqrt(HEAD_SIZE)

    def keys_values(u, shards):
        b, g = u // heads_kv, u % heads_kv
        k_bias = bias_row(QUERY_HEADS + mu * heads_kv + g)
        v_bias = bias_row(QUERY_HEADS + KEY_VALUE_HEADS + mu * heads_kv + g)
        lanes = pl.ds(pl.multiple_of(g * HEAD_SIZE, HEAD_SIZE), HEAD_SIZE)
        k_parts, v_parts = [], []
        for j in shards:
            x = k_buf[j, b, :, lanes].astype(jnp.float32) + k_bias
            k_parts.append(rotate(x, cos_t[b, j], sin_t[b, j]).astype(jnp.bfloat16))
            v_parts.append((v_buf[j, b, :, lanes].astype(jnp.float32) + v_bias).astype(jnp.bfloat16))
        if len(shards) == 1:
            return k_parts[0], v_parts[0]
        return jnp.concatenate(k_parts, axis=0), jnp.concatenate(v_parts, axis=0)

    def scores(u, i, k, mask):
        q = q_rot[u, i * rows : (i + heads_at_once) * rows, :]
        s = lax.dot_general(q, k, (((1,), (1,)), ((), ())), preferred_element_type=jnp.float32)
        return s.reshape(heads_at_once, rows, k.shape[0]) + mask[None]

    def blend(p, v):
        return jnp.dot(
            p.astype(jnp.bfloat16).reshape(heads_at_once * rows, v.shape[0]), v,
            preferred_element_type=jnp.float32,
        ).reshape(heads_at_once, rows, HEAD_SIZE)

    def compute_near(u):
        b = u // heads_kv
        k, v = keys_values(u, [off + k for k in range(n - 1)])
        mask = mask_near[b]
        for i in range(0, GROUP, heads_at_once):
            at = slice(i, i + heads_at_once)
            s = scores(u, i, k, mask)
            high = jnp.max(s, axis=-1, keepdims=True)
            p = jnp.exp2((s - high) * scale)
            high_buf[u, at] = high
            total_buf[u, at] = jnp.sum(p, axis=-1, keepdims=True)
            acc[u, at] = blend(p, v)

    def compute_far(u):
        b, g = u // heads_kv, u % heads_kv
        k, v = keys_values(u, [far])
        mask = mask_far[b]
        for i in range(0, GROUP, heads_at_once):
            at = slice(i, i + heads_at_once)
            s = scores(u, i, k, mask)
            before = high_buf[u, at]
            high = jnp.maximum(before, jnp.max(s, axis=-1, keepdims=True))
            p = jnp.exp2((s - high) * scale)
            shrink = jnp.exp2((before - high) * scale)
            total = total_buf[u, at] * shrink + jnp.sum(p, axis=-1, keepdims=True)
            o = acc[u, at] * shrink + blend(p, v)
            o = (o / total).astype(jnp.bfloat16)
            for e in range(heads_at_once):
                start = pl.multiple_of(g * wide + (i + e) * HEAD_SIZE, HEAD_SIZE)
                out_ref[b, :, pl.ds(start, HEAD_SIZE)] = o[e]

    def relay(c, want_far):
        for hop in range(1, n):
            right_is_far = (2 * me <= n - 1) & (me + hop == n - 1)
            left_is_far = (2 * me > n - 1) & (me - hop == 0)

            @pl.when((me + hop < n) & (right_is_far if want_far else ~right_is_far))
            def _():
                for copy in to_left(me + hop, c):
                    copy.wait_recv()

                @pl.when(me > 0)
                def _():
                    for copy in to_left(me + hop, c):
                        copy.start()

            @pl.when((me - hop >= 0) & (left_is_far if want_far else ~left_is_far))
            def _():
                for copy in to_right(me - hop, c):
                    copy.wait_recv()

                @pl.when(me < n - 1)
                def _():
                    for copy in to_right(me - hop, c):
                        copy.start()

    def phase(compute, want_far):
        @pl.loop(0, units)
        def _(u):
            for c, (b, g, _) in enumerate(chunks):
                @pl.when(u == b * heads_kv + g)
                def _():
                    relay(c, want_far)

            compute(u)

    phase(compute_near, False)
    phase(compute_far, True)

    for c in range(len(chunks)):
        for j in range(n):
            @pl.when((j <= me) & (me < n - 1))
            def _():
                for copy in to_right(j, c):
                    copy.wait_send()

            @pl.when((j >= me) & (me > 0))
            def _():
                for copy in to_left(j, c):
                    copy.wait_send()

    for j in range(n):
        @pl.when(j != me)
        def _():
            pos_copy(me, j).wait_send()

    @pl.when(me == 0)
    def _():
        for d in range(1, nf):
            bias_copy(mf, lax.rem(mf + d, nf)).wait_send()
        for j in range(1, n):
            spread_copy(j).wait_send()


def on_device(n, nf, q, k, v, bias, positions, rescale, table_index):
    batch, rows, width = q.shape
    heads_kv = k.shape[2] // HEAD_SIZE
    units = batch * heads_kv
    count = len(chunk_list(batch, heads_kv))
    bias = bias.reshape(-1, HEAD_SIZE)
    hbm = pl.BlockSpec(memory_space=pltpu.HBM)
    dma = pltpu.SemaphoreType.DMA
    f32, bf16 = jnp.float32, jnp.bfloat16
    return pl.pallas_call(
        functools.partial(kernel, n, nf, 8 if n <= 4 else 1),
        out_shape=jax.ShapeDtypeStruct(q.shape, bf16),
        in_specs=[hbm] * 7,
        out_specs=pl.BlockSpec(memory_space=pltpu.VMEM),
        scratch_shapes=[
            pltpu.SMEM(table_index.shape, jnp.int32),
            pltpu.VMEM((n,) + positions.shape, jnp.int32),
            pltpu.VMEM(rescale.shape, f32),
            dma((4,)),
            pltpu.VMEM((batch, rows, width), bf16),
            pltpu.VMEM((units, GROUP * rows, HEAD_SIZE), bf16),
            pltpu.VMEM((n,) + k.shape, bf16),
            pltpu.VMEM((n,) + v.shape, bf16),
            pltpu.VMEM((batch, n, rows, HEAD_SIZE), f32),
            pltpu.VMEM((batch, n, rows, HEAD_SIZE), f32),
            pltpu.VMEM((batch, rows, (n - 1) * rows), f32),
            pltpu.VMEM((batch, rows, rows), f32),
            pltpu.VMEM((nf,) + bias.shape, bf16),
            pltpu.VMEM((nf,) + bias.shape, f32),
            pltpu.VMEM((units, GROUP, rows, HEAD_SIZE), f32),
            pltpu.VMEM((units, GROUP, rows, 1), f32),
            pltpu.VMEM((units, GROUP, rows, 1), f32),
            dma((batch,)), dma((batch, 2)),
            dma((n, count, 2)), dma((n, count, 2)), dma((n, count, 2)),
            dma((n,)), dma((n,)), dma((nf,)), dma((nf,)), dma((n,)), dma,
            pltpu.SemaphoreType.REGULAR((n,)),
        ],
        compiler_params=pltpu.CompilerParams(
            collective_id=0, has_side_effects=True, vmem_limit_bytes=56 * 1024 * 1024
        ),
        name="relay_attention",
    )(*(pltpu.with_memory_space_constraint(x, pltpu.HBM) for x in (table_index, q, k, v, bias, positions, rescale)))


def solution(mesh):
    in_specs = (
        P("fsdp", "ctx", "uly"),
        P("fsdp", "ctx", "uly"),
        P("fsdp", "ctx", "uly"),
        P("fsdp"),
        P("fsdp", "ctx"),
        P(),
        P("fsdp"),
    )
    n, nf = mesh.shape["ctx"], mesh.shape["fsdp"]
    return jax.shard_map(
        functools.partial(on_device, n, nf),
        mesh=mesh, in_specs=in_specs, out_specs=P("fsdp", "ctx", "uly"), check_vma=False,
    )
```

```python
import functools
import math

import jax
import jax.numpy as jnp
from jax import lax
from jax.experimental import pallas as pl
from jax.experimental.pallas import tpu as pltpu
from jax.sharding import PartitionSpec as P

QUERY_HEADS = 64
KEY_VALUE_HEADS = 8
HEAD_SIZE = 128
GROUP = QUERY_HEADS // KEY_VALUE_HEADS
RUN = 48

rope_base = 1000000.0
masked_value = -1e30
MESH = pl.DeviceIdType.MESH


def sine_cosine(angle):
    turns = jnp.floor(angle * (2.0 / math.pi) + 0.5)
    r = angle - turns * 1.5703125
    r = r - turns * 4.837512969970703125e-4
    r = r - turns * 7.54978995489188216e-8
    z = r * r
    s = r + r * z * (-1.6666654611e-1 + z * (8.3321608736e-3 - z * 1.9515295891e-4))
    c = 1.0 - 0.5 * z + z * z * (
        4.166664568298827e-2 + z * (-1.388731625493765e-3 + z * 2.443315711809948e-5)
    )
    quarter = turns.astype(jnp.int32) & 3
    odd = (quarter & 1) == 1
    sine = jnp.where(odd, c, s)
    cosine = jnp.where(odd, s, c)
    sine = jnp.where(quarter >= 2, -sine, sine)
    cosine = jnp.where((quarter == 1) | (quarter == 2), -cosine, cosine)
    return sine, cosine


def piece_list(batch, heads_kv, split_last):
    groups = [(b, 0, heads_kv) for b in range(batch)]
    if split_last:
        groups = groups[:-1] + [(batch - 1, g, 1) for g in range(heads_kv)]
    return [group + (kind,) for group in groups for kind in (0, 1)]


def kernel(
    n, nf, heads_at_once,
    table_hbm, q_hbm, k_hbm, v_hbm, bias_hbm, pos_hbm, rescale_hbm,
    out_ref,
    table_ref, pos_buf, rescale_ref, small_sem,
    q_buf, q_rot, k_buf, v_buf, k_rot, v_all, cos_t, sin_t, mask_t, bias_buf, bias_f,
    q_sem, own_sem, send_right, send_left, recv_sem,
    pos_send, pos_recv, bias_send, bias_recv, spread_send, spread_recv, ready,
):
    batch, rows, _ = q_hbm.shape
    heads_kv = k_hbm.shape[2] // HEAD_SIZE
    units = batch * heads_kv
    me = lax.axis_index("ctx")
    mf = lax.axis_index("fsdp")
    mu = lax.axis_index("uly")
    shard_rows = bias_hbm.shape[0]
    ends = piece_list(batch, heads_kv, True)
    middle = piece_list(batch, heads_kv, False)
    wide = GROUP * HEAD_SIZE
    far = jnp.where(2 * me <= n - 1, n - 1, 0)

    barrier = pltpu.get_barrier_semaphore()

    @pl.when(me > 0)
    def _():
        pl.semaphore_wait(barrier, 1)

    @pl.when(me < n - 1)
    def _():
        pl.semaphore_signal(barrier, inc=1, device_id={"ctx": me + 1}, device_id_type=MESH)

    @pl.when(me == 0)
    def _():
        for d in range(1, nf):
            pl.semaphore_signal(
                barrier, inc=1, device_id={"fsdp": lax.rem(mf + d, nf)}, device_id_type=MESH
            )
        pl.semaphore_wait(barrier, nf - 1)

    def pos_copy(source, target):
        return pltpu.make_async_remote_copy(
            src_ref=pos_hbm, dst_ref=pos_buf.at[source],
            send_sem=pos_send.at[target], recv_sem=pos_recv.at[source],
            device_id={"ctx": target}, device_id_type=MESH,
        )

    def remote(shard, pieces, p, own, sems, target):
        b, g, heads, kind = pieces[p]
        lanes = pl.ds(g * HEAD_SIZE, heads * HEAD_SIZE)
        at = (b, slice(None), lanes)
        hbm, buf = ((k_hbm, k_buf), (v_hbm, v_buf))[kind]
        return pltpu.make_async_remote_copy(
            src_ref=hbm.at[at] if own else buf.at[(shard,) + at],
            dst_ref=buf.at[(shard,) + at],
            send_sem=sems.at[shard, p], recv_sem=recv_sem.at[shard, p],
            device_id={"ctx": target}, device_id_type=MESH,
        )

    def to_right(shard, pieces, p, own=False):
        return remote(shard, pieces, p, own, send_right, lax.rem(me + 1, n))

    def to_left(shard, pieces, p, own=False):
        return remote(shard, pieces, p, own, send_left, lax.rem(me + n - 1, n))

    @pl.when(me > 0)
    def _():
        for j in range(n - 1):
            @pl.when(j < me)
            def _():
                pos_copy(me, j).start()

    @pl.when(me == n - 1)
    def _():
        for p in range(len(ends)):
            to_left(me, ends, p, True).start()

    @pl.when((me > 0) & (me < n - 1))
    def _():
        for p in range(len(middle)):
            to_left(me, middle, p, True).start()

    for j in range(n - 1):
        @pl.when(j < me)
        def _():
            pl.semaphore_signal(
                ready.at[me], inc=1, device_id={"ctx": j}, device_id_type=MESH
            )

    small = [
        pltpu.make_async_copy(source, target, small_sem.at[i])
        for i, (source, target) in enumerate(
            (
                (pos_hbm, pos_buf.at[me]), (rescale_hbm, rescale_ref),
                (table_hbm, table_ref),
            )
        )
    ]
    own_bias = pltpu.make_async_copy(bias_hbm, bias_buf.at[mf], small_sem.at[3])
    for copy in small:
        copy.start()

    @pl.when(me == 0)
    def _():
        own_bias.start()

    def q_copy(b):
        return pltpu.make_async_copy(q_hbm.at[b], q_buf.at[b], q_sem.at[b])

    own = (
        pltpu.make_async_copy(k_hbm, k_buf.at[me], own_sem.at[0]),
        pltpu.make_async_copy(v_hbm, v_buf.at[me], own_sem.at[1]),
    )

    for b in range(batch):
        q_copy(b).start()
    for copy in own:
        copy.start()
    for copy in small:
        copy.wait()

    def bias_copy(source, target):
        return pltpu.make_async_remote_copy(
            src_ref=bias_hbm, dst_ref=bias_buf.at[source],
            send_sem=bias_send.at[target], recv_sem=bias_recv.at[source],
            device_id={"fsdp": target}, device_id_type=MESH,
        )

    def spread_copy(target):
        return pltpu.make_async_remote_copy(
            src_ref=bias_buf, dst_ref=bias_buf,
            send_sem=spread_send.at[target], recv_sem=spread_recv,
            device_id={"ctx": target}, device_id_type=MESH,
        )

    @pl.when(me == 0)
    def _():
        for d in range(1, nf):
            bias_copy(mf, lax.rem(mf + d, nf)).start()
        own_bias.wait()
        for d in range(1, nf):
            other = lax.rem(mf + d, nf)
            bias_copy(other, other).wait_recv()

    for j in range(1, n):
        @pl.when(me < j)
        def _():
            pl.semaphore_wait(ready.at[j], 1)
            pos_copy(me, j).start()

        @pl.when((me < j) & (me == 0))
        def _():
            spread_copy(j).start()

    @pl.when(me == 0)
    def _():
        for p in range(len(ends)):
            to_right(me, ends, p, True).start()

    @pl.when((me > 0) & (me < n - 1))
    def _():
        for p in range(len(middle)):
            to_right(me, middle, p, True).start()

    @pl.when(me > 0)
    def _():
        spread_copy(0).wait_recv()

    for f in range(nf):
        bias_f[f] = bias_buf[f].astype(jnp.float32)

    def bias_row(row):
        return bias_f[row // shard_rows, pl.ds(row % shard_rows, 1), :]

    for j in range(n):
        @pl.when(j != me)
        def _():
            pos_copy(j, j).wait_recv()

    lane = lax.broadcasted_iota(jnp.int32, (1, HEAD_SIZE), 1)
    power = jnp.exp(
        (lane % (HEAD_SIZE // 2)).astype(jnp.float32)
        * (2.0 / HEAD_SIZE * math.log(rope_base))
    )
    low_half = lane < HEAD_SIZE // 2
    run_rows = lax.broadcasted_iota(jnp.int32, (RUN, HEAD_SIZE), 0)
    query_row = lax.broadcasted_iota(jnp.int32, (RUN, 1), 0)
    keys = n * rows
    key_lane = lax.broadcasted_iota(jnp.int32, (1, keys), 1)

    for b in range(batch):
        factors = rescale_ref[0:1, :]
        for t in range(1, rescale_ref.shape[0]):
            factors = jnp.where(table_ref[b] == t, rescale_ref[t : t + 1, :], factors)
        inverse = 1.0 / (jnp.concatenate([factors, factors], axis=1) * power)
        key_pos = key_lane % RUN
        for j in range(n):
            for piece in range(rows // RUN):
                first = pos_buf[j, b : b + 1, piece * RUN : piece * RUN + 1]
                here = key_lane // RUN == j * (rows // RUN) + piece
                key_pos = key_pos + jnp.where(here, first, 0)
                place = (run_rows + first).astype(jnp.float32)
                sine, cosine = sine_cosine(place * inverse)
                block = slice(piece * RUN, (piece + 1) * RUN)
                cos_t[b, j, block, :] = cosine
                sin_t[b, j, block, :] = jnp.where(low_half, -sine, sine)
        for piece in range(rows // RUN):
            first = pos_buf[me, b : b + 1, piece * RUN : piece * RUN + 1]
            mask_t[b, piece * RUN : (piece + 1) * RUN, :] = jnp.where(
                key_pos <= query_row + first, 0.0, masked_value
            )

    def rotate(x, cosine, sine):
        return x * cosine + pltpu.roll(x, HEAD_SIZE // 2, 1) * sine

    scale = math.log2(math.e) / math.sqrt(HEAD_SIZE)
    query_heads_here = heads_kv * GROUP
    for b in range(batch):
        q_copy(b).wait()

        @pl.loop(0, heads_kv)
        def _(g):
            for i in range(GROUP):
                x = q_buf[
                    b, :, pl.ds(pl.multiple_of(g * wide + i * HEAD_SIZE, HEAD_SIZE), HEAD_SIZE)
                ].astype(jnp.float32)
                x = x + bias_row(mu * query_heads_here + g * GROUP + i)
                q_rot[b * heads_kv + g, i * rows : (i + 1) * rows, :] = (
                    rotate(x, cos_t[b, me], sin_t[b, me]) * scale
                ).astype(jnp.bfloat16)

    def prepare(u, j):
        b, g = u // heads_kv, u % heads_kv
        lanes = pl.ds(pl.multiple_of(g * HEAD_SIZE, HEAD_SIZE), HEAD_SIZE)
        x = k_buf[j, b, :, lanes].astype(jnp.float32)
        x = x + bias_row(QUERY_HEADS + mu * heads_kv + g)
        k_rot[u, j] = rotate(x, cos_t[b, j], sin_t[b, j]).astype(jnp.bfloat16)
        x = v_buf[j, b, :, lanes].astype(jnp.float32)
        x = x + bias_row(QUERY_HEADS + KEY_VALUE_HEADS + mu * heads_kv + g)
        v_all[u, j] = x.astype(jnp.bfloat16)

    def attend(u):
        prepare(u, far)
        b, g = u // heads_kv, u % heads_kv
        k = k_rot[u].reshape(keys, HEAD_SIZE)
        v = v_all[u].reshape(keys, HEAD_SIZE)
        mask = mask_t[b]
        for i in range(0, GROUP, heads_at_once):
            q = q_rot[u, i * rows : (i + heads_at_once) * rows, :]
            s = lax.dot_general(
                q, k, (((1,), (1,)), ((), ())), preferred_element_type=jnp.float32
            )
            s = s.reshape(heads_at_once, rows, keys) + mask[None]
            high = jnp.max(s, axis=-1, keepdims=True)
            p = jnp.exp2(s - high)
            total = jnp.sum(p, axis=-1, keepdims=True)
            o = jnp.dot(
                p.astype(jnp.bfloat16).reshape(heads_at_once * rows, keys), v,
                preferred_element_type=jnp.float32,
            ).reshape(heads_at_once, rows, HEAD_SIZE)
            o = (o / total).astype(jnp.bfloat16)
            for e in range(heads_at_once):
                start = pl.multiple_of(g * wide + (i + e) * HEAD_SIZE, HEAD_SIZE)
                out_ref[b, :, pl.ds(start, HEAD_SIZE)] = o[e]

    def pass_left(shard, pieces, p):
        to_left(shard, pieces, p).wait_recv()

        @pl.when(me > 0)
        def _():
            to_left(shard, pieces, p).start()

    def pass_right(shard, pieces, p):
        to_right(shard, pieces, p).wait_recv()

        @pl.when(me < n - 1)
        def _():
            to_right(shard, pieces, p).start()

    def of_entry(pieces, b):
        return [p for p, piece in enumerate(pieces) if piece[0] == b]

    def prepare_entry(b, j):
        @pl.loop(b * heads_kv, (b + 1) * heads_kv)
        def _(u):
            prepare(u, j)

    def take_near(b):
        for hop in range(1, n):
            right, left = me + hop, me - hop

            @pl.when((right < n) & (right != far))
            def _():
                @pl.when(right == n - 1)
                def _():
                    for p in of_entry(ends, b):
                        pass_left(right, ends, p)

                @pl.when(right < n - 1)
                def _():
                    for p in of_entry(middle, b):
                        pass_left(right, middle, p)

                prepare_entry(b, right)

            @pl.when((left >= 0) & (left != far))
            def _():
                @pl.when(left == 0)
                def _():
                    for p in of_entry(ends, b):
                        pass_right(left, ends, p)

                @pl.when(left > 0)
                def _():
                    for p in of_entry(middle, b):
                        pass_right(left, middle, p)

                prepare_entry(b, left)

    def pass_far(p):
        @pl.when(far > 0)
        def _():
            pass_left(far, ends, p)

        @pl.when(far == 0)
        def _():
            pass_right(far, ends, p)

    def take_far(first, last):
        @pl.loop(first * heads_kv, last * heads_kv)
        def _(u):
            for p, (b, g, _, _) in enumerate(ends):
                if first <= b < last:
                    @pl.when(u == b * heads_kv + g)
                    def _():
                        pass_far(p)

            attend(u)

    for copy in own:
        copy.wait()
    for b in range(batch):
        prepare_entry(b, me)
    for b in range(batch - 1):
        take_near(b)
    take_far(0, batch - 1)
    take_near(batch - 1)
    take_far(batch - 1, batch)

    for j in range(n):
        pieces = ends if j in (0, n - 1) else middle
        for p in range(len(pieces)):
            @pl.when((j <= me) & (me < n - 1))
            def _():
                to_right(j, pieces, p).wait_send()

            @pl.when((j >= me) & (me > 0))
            def _():
                to_left(j, pieces, p).wait_send()

    for j in range(n):
        @pl.when(j != me)
        def _():
            pos_copy(me, j).wait_send()

    @pl.when(me == 0)
    def _():
        for d in range(1, nf):
            bias_copy(mf, lax.rem(mf + d, nf)).wait_send()
        for j in range(1, n):
            spread_copy(j).wait_send()


def on_device(n, nf, q, k, v, bias, positions, rescale, table_index):
    batch, rows, width = q.shape
    heads_kv = k.shape[2] // HEAD_SIZE
    units = batch * heads_kv
    count = len(piece_list(batch, heads_kv, True))
    bias = bias.reshape(-1, HEAD_SIZE)
    hbm = pl.BlockSpec(memory_space=pltpu.HBM)
    dma = pltpu.SemaphoreType.DMA
    f32, bf16 = jnp.float32, jnp.bfloat16
    return pl.pallas_call(
        functools.partial(kernel, n, nf, 8 if n <= 4 else 1),
        out_shape=jax.ShapeDtypeStruct(q.shape, bf16),
        in_specs=[hbm] * 7,
        out_specs=pl.BlockSpec(memory_space=pltpu.VMEM),
        scratch_shapes=[
            pltpu.SMEM(table_index.shape, jnp.int32),
            pltpu.VMEM((n,) + positions.shape, jnp.int32),
            pltpu.VMEM(rescale.shape, f32),
            dma((4,)),
            pltpu.VMEM((batch, rows, width), bf16),
            pltpu.VMEM((units, GROUP * rows, HEAD_SIZE), bf16),
            pltpu.VMEM((n,) + k.shape, bf16),
            pltpu.VMEM((n,) + v.shape, bf16),
            pltpu.VMEM((units, n, rows, HEAD_SIZE), bf16),
            pltpu.VMEM((units, n, rows, HEAD_SIZE), bf16),
            pltpu.VMEM((batch, n, rows, HEAD_SIZE), f32),
            pltpu.VMEM((batch, n, rows, HEAD_SIZE), f32),
            pltpu.VMEM((batch, rows, n * rows), f32),
            pltpu.VMEM((nf,) + bias.shape, bf16),
            pltpu.VMEM((nf,) + bias.shape, f32),
            dma((batch,)), dma((2,)),
            dma((n, count)), dma((n, count)), dma((n, count)),
            dma((n,)), dma((n,)), dma((nf,)), dma((nf,)), dma((n,)), dma,
            pltpu.SemaphoreType.REGULAR((n,)),
        ],
        compiler_params=pltpu.CompilerParams(
            collective_id=0, has_side_effects=True, vmem_limit_bytes=48 * 1024 * 1024
        ),
        name="relay_attention",
    )(*(pltpu.with_memory_space_constraint(x, pltpu.HBM) for x in (table_index, q, k, v, bias, positions, rescale)))


def solution(mesh):
    in_specs = (
        P("fsdp", "ctx", "uly"),
        P("fsdp", "ctx", "uly"),
        P("fsdp", "ctx", "uly"),
        P("fsdp"),
        P("fsdp", "ctx"),
        P(),
        P("fsdp"),
    )
    n, nf = mesh.shape["ctx"], mesh.shape["fsdp"]
    return jax.shard_map(
        functools.partial(on_device, n, nf),
        mesh=mesh, in_specs=in_specs, out_specs=P("fsdp", "ctx", "uly"), check_vma=False,
    )
```

```python
import functools
import math

import jax
import jax.numpy as jnp
from jax import lax
from jax.experimental import pallas as pl
from jax.experimental.pallas import tpu as pltpu
from jax.sharding import PartitionSpec as P

QUERY_HEADS = 64
KEY_VALUE_HEADS = 8
HEAD_SIZE = 128
GROUP = QUERY_HEADS // KEY_VALUE_HEADS
RUN = 48

rope_base = 1000000.0
masked_value = -1e30
MESH = pl.DeviceIdType.MESH


def sine_cosine(angle):
    turns = jnp.floor(angle * (2.0 / math.pi) + 0.5)
    r = angle - turns * 1.5703125
    r = r - turns * 4.837512969970703125e-4
    r = r - turns * 7.54978995489188216e-8
    z = r * r
    s = r + r * z * (-1.6666654611e-1 + z * (8.3321608736e-3 - z * 1.9515295891e-4))
    c = 1.0 - 0.5 * z + z * z * (
        4.166664568298827e-2 + z * (-1.388731625493765e-3 + z * 2.443315711809948e-5)
    )
    quarter = turns.astype(jnp.int32) & 3
    odd = (quarter & 1) == 1
    sine = jnp.where(odd, c, s)
    cosine = jnp.where(odd, s, c)
    sine = jnp.where(quarter >= 2, -sine, sine)
    cosine = jnp.where((quarter == 1) | (quarter == 2), -cosine, cosine)
    return sine, cosine


def piece_list(batch, heads_kv, split_last):
    groups = [(b, 0, heads_kv) for b in range(batch)]
    if split_last:
        groups = groups[:-1] + [(batch - 1, g, 1) for g in range(heads_kv)]
    return [group + (kind,) for group in groups for kind in (0, 1)]


def attend_group(heads_at_once, q_ref, k_ref, v_ref, mask_ref, out_ref):
    shards, rows, _ = k_ref.shape
    keys = shards * rows
    scale = math.log2(math.e) / math.sqrt(HEAD_SIZE)
    k = k_ref[...].reshape(keys, HEAD_SIZE)
    v = v_ref[...].reshape(keys, HEAD_SIZE)
    mask = mask_ref[...]
    for i in range(0, GROUP, heads_at_once):
        q = q_ref[i * rows : (i + heads_at_once) * rows, :]
        s = lax.dot_general(
            q, k, (((1,), (1,)), ((), ())), preferred_element_type=jnp.float32
        )
        s = s.reshape(heads_at_once, rows, keys) + mask[None]
        high = jnp.max(s, axis=-1, keepdims=True)
        p = jnp.exp2((s - high) * scale)
        total = jnp.sum(p, axis=-1, keepdims=True)
        o = jnp.dot(
            p.astype(jnp.bfloat16).reshape(heads_at_once * rows, keys), v,
            preferred_element_type=jnp.float32,
        ).reshape(heads_at_once, rows, HEAD_SIZE)
        o = (o / total).astype(jnp.bfloat16)
        for e in range(heads_at_once):
            out_ref[:, (i + e) * HEAD_SIZE : (i + e + 1) * HEAD_SIZE] = o[e]


def write_kernel(heads_at_once, done_ref, q_ref, k_ref, v_ref, mask_ref, out_hbm, last, sems):
    batch = done_ref.shape[0]
    units, wide = q_ref.shape[0], last.shape[1]
    split = done_ref.shape[2] - wide
    copies = [
        pltpu.make_async_copy(done_ref.at[b], out_hbm.at[b], sems.at[b]) for b in range(batch - 1)
    ]
    if split:
        copies.append(pltpu.make_async_copy(
            done_ref.at[batch - 1, :, pl.ds(0, split)],
            out_hbm.at[batch - 1, :, pl.ds(0, split)], sems.at[batch - 1],
        ))
    for copy in copies:
        copy.start()
    u = units - 1
    attend_group(
        heads_at_once, q_ref.at[u], k_ref.at[u], v_ref.at[u], mask_ref.at[batch - 1], last
    )
    copy = pltpu.make_async_copy(
        last, out_hbm.at[batch - 1, :, pl.ds(split, wide)], sems.at[batch]
    )
    copy.start()
    for done in copies:
        done.wait()
    copy.wait()


def kernel(
    n, nf, heads_at_once,
    table_hbm, q_hbm, k_hbm, v_hbm, bias_hbm, pos_hbm, rescale_hbm,
    out_ref, q_rot, k_rot, v_all, mask_t,
    table_ref, pos_buf, rescale_ref, small_sem,
    q_buf, k_buf, v_buf, cos_t, sin_t, bias_buf, bias_f,
    q_sem, own_sem, send_right, send_left, recv_sem,
    pos_send, pos_recv, bias_send, bias_recv, spread_send, spread_recv, ready,
):
    batch, rows, _ = q_hbm.shape
    heads_kv = k_hbm.shape[2] // HEAD_SIZE
    units = batch * heads_kv
    me = lax.axis_index("ctx")
    mf = lax.axis_index("fsdp")
    mu = lax.axis_index("uly")
    shard_rows = bias_hbm.shape[0]
    ends = piece_list(batch, heads_kv, True)
    middle = piece_list(batch, heads_kv, False)
    wide = GROUP * HEAD_SIZE
    far = jnp.where(2 * me <= n - 1, n - 1, 0)

    barrier = pltpu.get_barrier_semaphore()

    @pl.when(me > 0)
    def _():
        pl.semaphore_wait(barrier, 1)

    @pl.when(me < n - 1)
    def _():
        pl.semaphore_signal(barrier, inc=1, device_id={"ctx": me + 1}, device_id_type=MESH)

    @pl.when(me == 0)
    def _():
        for d in range(1, nf):
            pl.semaphore_signal(
                barrier, inc=1, device_id={"fsdp": lax.rem(mf + d, nf)}, device_id_type=MESH
            )
        pl.semaphore_wait(barrier, nf - 1)

    def pos_copy(source, target):
        return pltpu.make_async_remote_copy(
            src_ref=pos_hbm, dst_ref=pos_buf.at[source],
            send_sem=pos_send.at[target], recv_sem=pos_recv.at[source],
            device_id={"ctx": target}, device_id_type=MESH,
        )

    def remote(shard, pieces, p, own, sems, target):
        b, g, heads, kind = pieces[p]
        lanes = pl.ds(g * HEAD_SIZE, heads * HEAD_SIZE)
        at = (b, slice(None), lanes)
        hbm, buf = ((k_hbm, k_buf), (v_hbm, v_buf))[kind]
        return pltpu.make_async_remote_copy(
            src_ref=hbm.at[at] if own else buf.at[(shard,) + at],
            dst_ref=buf.at[(shard,) + at],
            send_sem=sems.at[shard, p], recv_sem=recv_sem.at[shard, p],
            device_id={"ctx": target}, device_id_type=MESH,
        )

    def to_right(shard, pieces, p, own=False):
        return remote(shard, pieces, p, own, send_right, lax.rem(me + 1, n))

    def to_left(shard, pieces, p, own=False):
        return remote(shard, pieces, p, own, send_left, lax.rem(me + n - 1, n))

    for j in range(n - 1):
        @pl.when(j < me)
        def _():
            pl.semaphore_signal(
                ready.at[me], inc=1, device_id={"ctx": j}, device_id_type=MESH
            )

    @pl.when(me > 0)
    def _():
        for j in range(n - 1):
            @pl.when(j < me)
            def _():
                pos_copy(me, j).start()

    @pl.when(me == n - 1)
    def _():
        for p in range(len(ends)):
            to_left(me, ends, p, True).start()

    @pl.when((me > 0) & (me < n - 1))
    def _():
        for p in range(len(middle)):
            to_left(me, middle, p, True).start()

    small = [
        pltpu.make_async_copy(source, target, small_sem.at[i])
        for i, (source, target) in enumerate(
            (
                (pos_hbm, pos_buf.at[me]), (rescale_hbm, rescale_ref),
                (table_hbm, table_ref),
            )
        )
    ]
    own_bias = pltpu.make_async_copy(bias_hbm, bias_buf.at[mf], small_sem.at[3])
    for copy in small:
        copy.start()

    @pl.when(me == 0)
    def _():
        own_bias.start()

    def q_copy(b):
        return pltpu.make_async_copy(q_hbm.at[b], q_buf.at[b], q_sem.at[b])

    own = (
        pltpu.make_async_copy(k_hbm, k_buf.at[me], own_sem.at[0]),
        pltpu.make_async_copy(v_hbm, v_buf.at[me], own_sem.at[1]),
    )

    for copy in own:
        copy.start()
    def bias_copy(source, target):
        return pltpu.make_async_remote_copy(
            src_ref=bias_hbm, dst_ref=bias_buf.at[source],
            send_sem=bias_send.at[target], recv_sem=bias_recv.at[source],
            device_id={"fsdp": target}, device_id_type=MESH,
        )

    def spread_copy(target):
        return pltpu.make_async_remote_copy(
            src_ref=bias_buf, dst_ref=bias_buf,
            send_sem=spread_send.at[target], recv_sem=spread_recv,
            device_id={"ctx": target}, device_id_type=MESH,
        )

    @pl.when(me == 0)
    def _():
        for d in range(1, nf):
            bias_copy(mf, lax.rem(mf + d, nf)).start()
        own_bias.wait()
        for d in range(1, nf):
            other = lax.rem(mf + d, nf)
            bias_copy(other, other).wait_recv()

    for j in range(1, n):
        @pl.when(me < j)
        def _():
            pl.semaphore_wait(ready.at[j], 1)
            pos_copy(me, j).start()

        @pl.when((me < j) & (me == 0))
        def _():
            spread_copy(j).start()

    @pl.when(me == 0)
    def _():
        for p in range(len(ends)):
            to_right(me, ends, p, True).start()

    @pl.when((me > 0) & (me < n - 1))
    def _():
        for p in range(len(middle)):
            to_right(me, middle, p, True).start()

    for b in range(batch):
        q_copy(b).start()
    for copy in small:
        copy.wait()

    @pl.when(me > 0)
    def _():
        spread_copy(0).wait_recv()

    for f in range(nf):
        bias_f[f] = bias_buf[f].astype(jnp.float32)

    def bias_row(row):
        return bias_f[row // shard_rows, pl.ds(row % shard_rows, 1), :]

    for j in range(n):
        @pl.when(j != me)
        def _():
            pos_copy(j, j).wait_recv()

    lane = lax.broadcasted_iota(jnp.int32, (1, HEAD_SIZE), 1)
    power = jnp.exp(
        (lane % (HEAD_SIZE // 2)).astype(jnp.float32)
        * (2.0 / HEAD_SIZE * math.log(rope_base))
    )
    low_half = lane < HEAD_SIZE // 2
    run_rows = lax.broadcasted_iota(jnp.int32, (RUN, HEAD_SIZE), 0)
    query_row = lax.broadcasted_iota(jnp.int32, (RUN, 1), 0)
    keys = n * rows
    key_lane = lax.broadcasted_iota(jnp.int32, (1, keys), 1)

    for b in range(batch):
        factors = rescale_ref[0:1, :]
        for t in range(1, rescale_ref.shape[0]):
            factors = jnp.where(table_ref[b] == t, rescale_ref[t : t + 1, :], factors)
        inverse = 1.0 / (jnp.concatenate([factors, factors], axis=1) * power)
        key_pos = key_lane % RUN
        for j in range(n):
            for piece in range(rows // RUN):
                first = pos_buf[j, b : b + 1, piece * RUN : piece * RUN + 1]
                here = key_lane // RUN == j * (rows // RUN) + piece
                key_pos = key_pos + jnp.where(here, first, 0)
                place = (run_rows + first).astype(jnp.float32)
                sine, cosine = sine_cosine(place * inverse)
                block = slice(piece * RUN, (piece + 1) * RUN)
                cos_t[b, j, block, :] = cosine
                sin_t[b, j, block, :] = jnp.where(low_half, -sine, sine)
        for piece in range(rows // RUN):
            first = pos_buf[me, b : b + 1, piece * RUN : piece * RUN + 1]
            mask_t[b, piece * RUN : (piece + 1) * RUN, :] = jnp.where(
                key_pos <= query_row + first, 0.0, masked_value
            )

    def rotate(x, cosine, sine):
        return x * cosine + pltpu.roll(x, HEAD_SIZE // 2, 1) * sine

    query_heads_here = heads_kv * GROUP

    def rotate_queries(b):
        q_copy(b).wait()

        @pl.loop(0, heads_kv)
        def _(g):
            for i in range(GROUP):
                x = q_buf[
                    b, :, pl.ds(pl.multiple_of(g * wide + i * HEAD_SIZE, HEAD_SIZE), HEAD_SIZE)
                ].astype(jnp.float32)
                x = x + bias_row(mu * query_heads_here + g * GROUP + i)
                q_rot[b * heads_kv + g, i * rows : (i + 1) * rows, :] = rotate(
                    x, cos_t[b, me], sin_t[b, me]
                ).astype(jnp.bfloat16)

    def prepare(u, j):
        b, g = u // heads_kv, u % heads_kv
        lanes = pl.ds(pl.multiple_of(g * HEAD_SIZE, HEAD_SIZE), HEAD_SIZE)
        x = k_buf[j, b, :, lanes].astype(jnp.float32)
        x = x + bias_row(QUERY_HEADS + mu * heads_kv + g)
        k_rot[u, j] = rotate(x, cos_t[b, j], sin_t[b, j]).astype(jnp.bfloat16)
        x = v_buf[j, b, :, lanes].astype(jnp.float32)
        x = x + bias_row(QUERY_HEADS + KEY_VALUE_HEADS + mu * heads_kv + g)
        v_all[u, j] = x.astype(jnp.bfloat16)

    def attend(u):
        b, g = u // heads_kv, u % heads_kv
        attend_group(
            heads_at_once, q_rot.at[u], k_rot.at[u], v_all.at[u], mask_t.at[b],
            out_ref.at[b, :, pl.ds(pl.multiple_of(g * wide, wide), wide)],
        )

    def pass_left(shard, pieces, p):
        to_left(shard, pieces, p).wait_recv()

        @pl.when(me > 0)
        def _():
            to_left(shard, pieces, p).start()

    def pass_right(shard, pieces, p):
        to_right(shard, pieces, p).wait_recv()

        @pl.when(me < n - 1)
        def _():
            to_right(shard, pieces, p).start()

    def of_entry(pieces, b):
        return [p for p, piece in enumerate(pieces) if piece[0] == b]

    def prepare_entry(b, j):
        @pl.loop(b * heads_kv, (b + 1) * heads_kv)
        def _(u):
            prepare(u, j)

    def each_near(act):
        for hop in range(1, n):
            right, left = me + hop, me - hop

            @pl.when((right < n) & (right != far))
            def _():
                act(right, pass_left, right == n - 1)

            @pl.when((left >= 0) & (left != far))
            def _():
                act(left, pass_right, left == 0)

    def pass_near(b):
        def act(shard, hand_on, at_end):
            for pieces, chosen in ((ends, at_end), (middle, ~at_end)):
                @pl.when(chosen)
                def _():
                    for p in of_entry(pieces, b):
                        hand_on(shard, pieces, p)

        each_near(act)

    def prepare_near(b):
        each_near(lambda shard, hand_on, at_end: prepare_entry(b, shard))

    inner = (me > 0) & (me < n - 1)

    def pass_far(p):
        to_left(far, ends, p).wait_recv()

        @pl.when(inner & (far > 0))
        def _():
            to_left(far, ends, p).start()

        @pl.when(inner & (far == 0))
        def _():
            to_right(far, ends, p).start()

    def take_far(b):
        steps = {}
        for p in of_entry(ends, b):
            steps.setdefault(ends[p][1], []).append(p)
        starts = sorted(steps) + [heads_kv]
        for first, last in zip(starts, starts[1:]):
            for p in steps[first]:
                pass_far(p)
            if last - first > 1:
                @pl.loop(b * heads_kv + first, b * heads_kv + last)
                def _(u):
                    prepare(u, far)
                    attend(u)
            else:
                prepare(b * heads_kv + first, far)
                if b * heads_kv + last < units:
                    attend(b * heads_kv + first)

    def wait_small_sends():
        for j in range(n):
            @pl.when(j != me)
            def _():
                pos_copy(me, j).wait_send()

        @pl.when(me == 0)
        def _():
            for d in range(1, nf):
                bias_copy(mf, lax.rem(mf + d, nf)).wait_send()
            for j in range(1, n):
                spread_copy(j).wait_send()

    def wait_end_sends():
        @pl.when(me == 0)
        def _():
            for p in range(len(ends)):
                to_right(me, ends, p).wait_send()

        @pl.when(me == n - 1)
        def _():
            for p in range(len(ends)):
                to_left(me, ends, p).wait_send()

    def wait_inner_sends():
        @pl.when(inner)
        def _():
            for j in range(n):
                pieces = ends if j in (0, n - 1) else middle
                for p in range(len(pieces)):
                    @pl.when(j <= me)
                    def _():
                        to_right(j, pieces, p).wait_send()

                    @pl.when(j >= me)
                    def _():
                        to_left(j, pieces, p).wait_send()

    rotate_queries(0)
    pass_near(0)
    for b in range(1, batch):
        rotate_queries(b)
        if b < batch - 1:
            pass_near(b)
    for copy in own:
        copy.wait()
    for b in range(batch):
        prepare_entry(b, me)
    for b in range(batch - 1):
        prepare_near(b)
    for b in range(batch - 1):
        take_far(b)
    pass_near(batch - 1)
    prepare_near(batch - 1)
    wait_small_sends()
    wait_end_sends()
    take_far(batch - 1)
    wait_inner_sends()


def on_device(n, nf, q, k, v, bias, positions, rescale, table_index):
    batch, rows, width = q.shape
    heads_kv = k.shape[2] // HEAD_SIZE
    units = batch * heads_kv
    count = len(piece_list(batch, heads_kv, True))
    bias = bias.reshape(-1, HEAD_SIZE)
    hbm = pl.BlockSpec(memory_space=pltpu.HBM)
    dma = pltpu.SemaphoreType.DMA
    f32, bf16 = jnp.float32, jnp.bfloat16
    vmem = pl.BlockSpec(memory_space=pltpu.VMEM)
    heads_at_once = 8 if n <= 4 else 1
    results = pl.pallas_call(
        functools.partial(kernel, n, nf, heads_at_once),
        out_shape=[
            jax.ShapeDtypeStruct(q.shape, bf16),
            jax.ShapeDtypeStruct((units, GROUP * rows, HEAD_SIZE), bf16),
            jax.ShapeDtypeStruct((units, n, rows, HEAD_SIZE), bf16),
            jax.ShapeDtypeStruct((units, n, rows, HEAD_SIZE), bf16),
            jax.ShapeDtypeStruct((batch, rows, n * rows), f32),
        ],
        in_specs=[hbm] * 7,
        out_specs=[vmem] * 5,
        scratch_shapes=[
            pltpu.SMEM(table_index.shape, jnp.int32),
            pltpu.VMEM((n,) + positions.shape, jnp.int32),
            pltpu.VMEM(rescale.shape, f32),
            dma((4,)),
            pltpu.VMEM((batch, rows, width), bf16),
            pltpu.VMEM((n,) + k.shape, bf16),
            pltpu.VMEM((n,) + v.shape, bf16),
            pltpu.VMEM((batch, n, rows, HEAD_SIZE), f32),
            pltpu.VMEM((batch, n, rows, HEAD_SIZE), f32),
            pltpu.VMEM((nf,) + bias.shape, bf16),
            pltpu.VMEM((nf,) + bias.shape, f32),
            dma((batch,)), dma((2,)),
            dma((n, count)), dma((n, count)), dma((n, count)),
            dma((n,)), dma((n,)), dma((nf,)), dma((nf,)), dma((n,)), dma,
            pltpu.SemaphoreType.REGULAR((n,)),
        ],
        compiler_params=pltpu.CompilerParams(
            collective_id=0, has_side_effects=True, vmem_limit_bytes=32 * 1024 * 1024
        ),
        name="relay_attention",
    )(*(pltpu.with_memory_space_constraint(x, pltpu.HBM) for x in (table_index, q, k, v, bias, positions, rescale)))
    return pl.pallas_call(
        functools.partial(write_kernel, heads_at_once),
        out_shape=jax.ShapeDtypeStruct(q.shape, bf16),
        in_specs=[vmem] * 5,
        out_specs=hbm,
        scratch_shapes=[pltpu.VMEM((rows, GROUP * HEAD_SIZE), bf16), dma((batch + 1,))],
        compiler_params=pltpu.CompilerParams(vmem_limit_bytes=24 * 1024 * 1024),
        name="write_result",
    )(*results)


def solution(mesh):
    in_specs = (
        P("fsdp", "ctx", "uly"),
        P("fsdp", "ctx", "uly"),
        P("fsdp", "ctx", "uly"),
        P("fsdp"),
        P("fsdp", "ctx"),
        P(),
        P("fsdp"),
    )
    n, nf = mesh.shape["ctx"], mesh.shape["fsdp"]
    return jax.shard_map(
        functools.partial(on_device, n, nf),
        mesh=mesh, in_specs=in_specs, out_specs=P("fsdp", "ctx", "uly"), check_vma=False,
    )
```

```python
import functools
import math

import jax
import jax.numpy as jnp
from jax import lax
from jax.experimental import pallas as pl
from jax.experimental.pallas import tpu as pltpu
from jax.sharding import PartitionSpec as P

QUERY_HEADS = 64
KEY_VALUE_HEADS = 8
HEAD_SIZE = 128
GROUP = QUERY_HEADS // KEY_VALUE_HEADS
RUN = 48

rope_base = 1000000.0
masked_value = -1e30
MESH = pl.DeviceIdType.MESH


def sine_cosine(angle):
    turns = jnp.floor(angle * (2.0 / math.pi) + 0.5)
    r = angle - turns * 1.5703125
    r = r - turns * 4.837512969970703125e-4
    r = r - turns * 7.54978995489188216e-8
    z = r * r
    s = r + r * z * (-1.6666654611e-1 + z * (8.3321608736e-3 - z * 1.9515295891e-4))
    c = 1.0 - 0.5 * z + z * z * (
        4.166664568298827e-2 + z * (-1.388731625493765e-3 + z * 2.443315711809948e-5)
    )
    quarter = turns.astype(jnp.int32) & 3
    odd = (quarter & 1) == 1
    sine = jnp.where(odd, c, s)
    cosine = jnp.where(odd, s, c)
    sine = jnp.where(quarter >= 2, -sine, sine)
    cosine = jnp.where((quarter == 1) | (quarter == 2), -cosine, cosine)
    return sine, cosine


def piece_list(batch, heads_kv, split_last):
    groups = [(b, 0, heads_kv) for b in range(batch)]
    if split_last:
        groups = groups[:-1] + [(batch - 1, g, 1) for g in range(heads_kv)]
    return [group + (kind,) for group in groups for kind in (0, 1)]


def attend_group(heads_at_once, q_ref, k_ref, v_ref, mask_ref, out_ref):
    shards, rows, _ = k_ref.shape
    keys = shards * rows
    scale = math.log2(math.e) / math.sqrt(HEAD_SIZE)
    k = k_ref[...].reshape(keys, HEAD_SIZE)
    v = v_ref[...].reshape(keys, HEAD_SIZE)
    mask = mask_ref[...]
    for i in range(0, GROUP, heads_at_once):
        q = q_ref[i * rows : (i + heads_at_once) * rows, :]
        s = lax.dot_general(
            q, k, (((1,), (1,)), ((), ())), preferred_element_type=jnp.float32
        )
        s = s.reshape(heads_at_once, rows, keys) + mask[None]
        high = jnp.max(s, axis=-1, keepdims=True)
        p = jnp.exp2((s - high) * scale)
        total = jnp.sum(p, axis=-1, keepdims=True)
        o = jnp.dot(
            p.astype(jnp.bfloat16).reshape(heads_at_once * rows, keys), v,
            preferred_element_type=jnp.float32,
        ).reshape(heads_at_once, rows, HEAD_SIZE)
        o = (o / total).astype(jnp.bfloat16)
        for e in range(heads_at_once):
            out_ref[:, (i + e) * HEAD_SIZE : (i + e + 1) * HEAD_SIZE] = o[e]


def write_kernel(heads_at_once, done_ref, q_ref, k_ref, v_ref, mask_ref, out_hbm, last, sems):
    batch = done_ref.shape[0]
    units, wide = q_ref.shape[0], last.shape[1]
    split = done_ref.shape[2] - wide
    copies = [
        pltpu.make_async_copy(done_ref.at[b], out_hbm.at[b], sems.at[b]) for b in range(batch - 1)
    ]
    if split:
        copies.append(pltpu.make_async_copy(
            done_ref.at[batch - 1, :, pl.ds(0, split)],
            out_hbm.at[batch - 1, :, pl.ds(0, split)], sems.at[batch - 1],
        ))
    for copy in copies:
        copy.start()
    u = units - 1
    attend_group(
        heads_at_once, q_ref.at[u], k_ref.at[u], v_ref.at[u], mask_ref.at[batch - 1], last
    )
    copy = pltpu.make_async_copy(
        last, out_hbm.at[batch - 1, :, pl.ds(split, wide)], sems.at[batch]
    )
    copy.start()
    for done in copies:
        done.wait()
    copy.wait()


def kernel(
    n, nf, heads_at_once,
    table_hbm, q_hbm, k_hbm, v_hbm, bias_hbm, pos_hbm, rescale_hbm,
    out_ref, q_rot, k_rot, v_all, mask_t,
    table_ref, pos_buf, rescale_ref, small_sem,
    q_buf, k_buf, v_buf, cos_t, sin_t, bias_buf, bias_f,
    q_sem, own_sem, send_right, send_left, recv_sem,
    pos_send, pos_recv, bias_send, bias_recv, spread_send, spread_recv, ready, turn,
):
    batch, rows, _ = q_hbm.shape
    heads_kv = k_hbm.shape[2] // HEAD_SIZE
    units = batch * heads_kv
    me = lax.axis_index("ctx")
    mf = lax.axis_index("fsdp")
    mu = lax.axis_index("uly")
    shard_rows = bias_hbm.shape[0]
    ends = piece_list(batch, heads_kv, True)
    middle = piece_list(batch, heads_kv, False)
    wide = GROUP * HEAD_SIZE
    far = jnp.where(2 * me <= n - 1, n - 1, 0)

    barrier = pltpu.get_barrier_semaphore()

    inner = (me > 0) & (me < n - 1)
    even = mf % 2 == 0

    @pl.when(inner & ~even)
    def _():
        pl.semaphore_signal(barrier, inc=1, device_id={"fsdp": mf - 1}, device_id_type=MESH)

    @pl.when(inner & even)
    def _():
        pl.semaphore_wait(barrier, 2)

    @pl.when((inner & ~even) | (me == n - 1))
    def _():
        pl.semaphore_wait(barrier, 1)

    @pl.when(me < n - 1)
    def _():
        pl.semaphore_signal(barrier, inc=1, device_id={"ctx": me + 1}, device_id_type=MESH)

    @pl.when(me == 0)
    def _():
        for d in range(1, nf):
            pl.semaphore_signal(
                barrier, inc=1, device_id={"fsdp": lax.rem(mf + d, nf)}, device_id_type=MESH
            )
        pl.semaphore_wait(barrier, nf - 1)

    def pos_copy(source, target):
        return pltpu.make_async_remote_copy(
            src_ref=pos_hbm, dst_ref=pos_buf.at[source],
            send_sem=pos_send.at[target], recv_sem=pos_recv.at[source],
            device_id={"ctx": target}, device_id_type=MESH,
        )

    def remote(shard, pieces, p, own, sems, target):
        b, g, heads, kind = pieces[p]
        lanes = pl.ds(g * HEAD_SIZE, heads * HEAD_SIZE)
        at = (b, slice(None), lanes)
        hbm, buf = ((k_hbm, k_buf), (v_hbm, v_buf))[kind]
        return pltpu.make_async_remote_copy(
            src_ref=hbm.at[at] if own else buf.at[(shard,) + at],
            dst_ref=buf.at[(shard,) + at],
            send_sem=sems.at[shard, p], recv_sem=recv_sem.at[shard, p],
            device_id={"ctx": target}, device_id_type=MESH,
        )

    def to_right(shard, pieces, p, own=False):
        return remote(shard, pieces, p, own, send_right, lax.rem(me + 1, n))

    def to_left(shard, pieces, p, own=False):
        return remote(shard, pieces, p, own, send_left, lax.rem(me + n - 1, n))

    for j in range(n - 1):
        @pl.when(j < me)
        def _():
            pl.semaphore_signal(
                ready.at[me], inc=1, device_id={"ctx": j}, device_id_type=MESH
            )

    @pl.when(me > 0)
    def _():
        for j in range(n - 1):
            @pl.when(j < me)
            def _():
                pos_copy(me, j).start()

    @pl.when(me == n - 1)
    def _():
        for p in range(len(ends)):
            to_left(me, ends, p, True).start()

    @pl.when((me > 0) & (me < n - 1))
    def _():
        for p in range(len(middle)):
            to_left(me, middle, p, True).start()

    small = [
        pltpu.make_async_copy(source, target, small_sem.at[i])
        for i, (source, target) in enumerate(
            (
                (pos_hbm, pos_buf.at[me]), (rescale_hbm, rescale_ref),
                (table_hbm, table_ref),
            )
        )
    ]
    own_bias = pltpu.make_async_copy(bias_hbm, bias_buf.at[mf], small_sem.at[3])
    for copy in small:
        copy.start()

    @pl.when(me == 0)
    def _():
        own_bias.start()

    def q_copy(b):
        return pltpu.make_async_copy(q_hbm.at[b], q_buf.at[b], q_sem.at[b])

    own = (
        pltpu.make_async_copy(k_hbm, k_buf.at[me], own_sem.at[0]),
        pltpu.make_async_copy(v_hbm, v_buf.at[me], own_sem.at[1]),
    )

    for copy in own:
        copy.start()
    def bias_copy(source, target):
        return pltpu.make_async_remote_copy(
            src_ref=bias_hbm, dst_ref=bias_buf.at[source],
            send_sem=bias_send.at[target], recv_sem=bias_recv.at[source],
            device_id={"fsdp": target}, device_id_type=MESH,
        )

    def spread_copy(target):
        return pltpu.make_async_remote_copy(
            src_ref=bias_buf, dst_ref=bias_buf,
            send_sem=spread_send.at[target], recv_sem=spread_recv,
            device_id={"ctx": target}, device_id_type=MESH,
        )

    @pl.when(me == 0)
    def _():
        for d in range(1, nf):
            bias_copy(mf, lax.rem(mf + d, nf)).start()
        own_bias.wait()
        for d in range(1, nf):
            other = lax.rem(mf + d, nf)
            bias_copy(other, other).wait_recv()

    for j in range(1, n):
        @pl.when(me < j)
        def _():
            pl.semaphore_wait(ready.at[j], 1)
            pos_copy(me, j).start()

        @pl.when((me < j) & (me == 0))
        def _():
            spread_copy(j).start()

    @pl.when(me == 0)
    def _():
        for p in range(len(ends)):
            to_right(me, ends, p, True).start()

    @pl.when((me > 0) & (me < n - 1))
    def _():
        for p in range(len(middle)):
            to_right(me, middle, p, True).start()

    for b in range(batch):
        q_copy(b).start()
    for copy in small:
        copy.wait()

    @pl.when(me > 0)
    def _():
        spread_copy(0).wait_recv()

    for f in range(nf):
        bias_f[f] = bias_buf[f].astype(jnp.float32)

    def bias_row(row):
        return bias_f[row // shard_rows, pl.ds(row % shard_rows, 1), :]

    for j in range(n):
        @pl.when(j != me)
        def _():
            pos_copy(j, j).wait_recv()

    lane = lax.broadcasted_iota(jnp.int32, (1, HEAD_SIZE), 1)
    power = jnp.exp(
        (lane % (HEAD_SIZE // 2)).astype(jnp.float32)
        * (2.0 / HEAD_SIZE * math.log(rope_base))
    )
    low_half = lane < HEAD_SIZE // 2
    run_rows = lax.broadcasted_iota(jnp.int32, (RUN, HEAD_SIZE), 0)
    query_row = lax.broadcasted_iota(jnp.int32, (RUN, 1), 0)
    keys = n * rows
    key_lane = lax.broadcasted_iota(jnp.int32, (1, keys), 1)

    for b in range(batch):
        factors = rescale_ref[0:1, :]
        for t in range(1, rescale_ref.shape[0]):
            factors = jnp.where(table_ref[b] == t, rescale_ref[t : t + 1, :], factors)
        inverse = 1.0 / (jnp.concatenate([factors, factors], axis=1) * power)
        key_pos = key_lane % RUN
        for j in range(n):
            for piece in range(rows // RUN):
                first = pos_buf[j, b : b + 1, piece * RUN : piece * RUN + 1]
                here = key_lane // RUN == j * (rows // RUN) + piece
                key_pos = key_pos + jnp.where(here, first, 0)
                place = (run_rows + first).astype(jnp.float32)
                sine, cosine = sine_cosine(place * inverse)
                block = slice(piece * RUN, (piece + 1) * RUN)
                cos_t[b, j, block, :] = cosine
                sin_t[b, j, block, :] = jnp.where(low_half, -sine, sine)
        for piece in range(rows // RUN):
            first = pos_buf[me, b : b + 1, piece * RUN : piece * RUN + 1]
            mask_t[b, piece * RUN : (piece + 1) * RUN, :] = jnp.where(
                key_pos <= query_row + first, 0.0, masked_value
            )

    def rotate(x, cosine, sine):
        return x * cosine + pltpu.roll(x, HEAD_SIZE // 2, 1) * sine

    query_heads_here = heads_kv * GROUP

    def rotate_queries(b):
        q_copy(b).wait()

        @pl.loop(0, heads_kv)
        def _(g):
            for i in range(GROUP):
                x = q_buf[
                    b, :, pl.ds(pl.multiple_of(g * wide + i * HEAD_SIZE, HEAD_SIZE), HEAD_SIZE)
                ].astype(jnp.float32)
                x = x + bias_row(mu * query_heads_here + g * GROUP + i)
                q_rot[b * heads_kv + g, i * rows : (i + 1) * rows, :] = rotate(
                    x, cos_t[b, me], sin_t[b, me]
                ).astype(jnp.bfloat16)

    def prepare(u, j):
        b, g = u // heads_kv, u % heads_kv
        lanes = pl.ds(pl.multiple_of(g * HEAD_SIZE, HEAD_SIZE), HEAD_SIZE)
        x = k_buf[j, b, :, lanes].astype(jnp.float32)
        x = x + bias_row(QUERY_HEADS + mu * heads_kv + g)
        k_rot[u, j] = rotate(x, cos_t[b, j], sin_t[b, j]).astype(jnp.bfloat16)
        x = v_buf[j, b, :, lanes].astype(jnp.float32)
        x = x + bias_row(QUERY_HEADS + KEY_VALUE_HEADS + mu * heads_kv + g)
        v_all[u, j] = x.astype(jnp.bfloat16)

    def attend(u):
        b, g = u // heads_kv, u % heads_kv
        attend_group(
            heads_at_once, q_rot.at[u], k_rot.at[u], v_all.at[u], mask_t.at[b],
            out_ref.at[b, :, pl.ds(pl.multiple_of(g * wide, wide), wide)],
        )

    def pass_left(shard, pieces, p):
        to_left(shard, pieces, p).wait_recv()

        @pl.when(me > 0)
        def _():
            to_left(shard, pieces, p).start()

    def pass_right(shard, pieces, p):
        to_right(shard, pieces, p).wait_recv()

        @pl.when(me < n - 1)
        def _():
            to_right(shard, pieces, p).start()

    def of_entry(pieces, b):
        return [p for p, piece in enumerate(pieces) if piece[0] == b]

    def prepare_entry(b, j):
        @pl.loop(b * heads_kv, (b + 1) * heads_kv)
        def _(u):
            prepare(u, j)

    def each_near(act):
        for hop in range(1, n):
            right, left = me + hop, me - hop

            @pl.when((right < n) & (right != far))
            def _():
                act(right, pass_left, right == n - 1)

            @pl.when((left >= 0) & (left != far))
            def _():
                act(left, pass_right, left == 0)

    def pass_near(b):
        def act(shard, hand_on, at_end):
            for pieces, chosen in ((ends, at_end), (middle, ~at_end)):
                @pl.when(chosen)
                def _():
                    for p in of_entry(pieces, b):
                        hand_on(shard, pieces, p)

        each_near(act)

    def prepare_near(b):
        each_near(lambda shard, hand_on, at_end: prepare_entry(b, shard))

    def pass_far(p):
        to_left(far, ends, p).wait_recv()

        @pl.when(inner & (far > 0))
        def _():
            to_left(far, ends, p).start()

        @pl.when(inner & (far == 0))
        def _():
            to_right(far, ends, p).start()

    marker = of_entry(middle, batch - 2)[-1]

    def hold_odd():
        @pl.when(inner & ~even)
        def _():
            pl.semaphore_wait(turn, 1)

    def release_odd():
        @pl.when(inner & even)
        def _():
            @pl.when(far > 0)
            def _():
                to_left(n - 2, middle, marker).wait_send()

            @pl.when(far == 0)
            def _():
                to_right(1, middle, marker).wait_send()

            pl.semaphore_signal(turn, inc=1, device_id={"fsdp": mf + 1}, device_id_type=MESH)

    def take_far(b):
        steps = {}
        for p in of_entry(ends, b):
            steps.setdefault(ends[p][1], []).append(p)
        starts = sorted(steps) + [heads_kv]
        for first, last in zip(starts, starts[1:]):
            if b == 0:
                hold_odd()
            for p in steps[first]:
                pass_far(p)
            if b == 0:
                release_odd()
            if last - first > 1:
                @pl.loop(b * heads_kv + first, b * heads_kv + last)
                def _(u):
                    prepare(u, far)
                    attend(u)
            else:
                prepare(b * heads_kv + first, far)
                if b * heads_kv + last < units:
                    attend(b * heads_kv + first)

    def wait_small_sends():
        for j in range(n):
            @pl.when(j != me)
            def _():
                pos_copy(me, j).wait_send()

        @pl.when(me == 0)
        def _():
            for d in range(1, nf):
                bias_copy(mf, lax.rem(mf + d, nf)).wait_send()
            for j in range(1, n):
                spread_copy(j).wait_send()

    def wait_end_sends():
        @pl.when(me == 0)
        def _():
            for p in range(len(ends)):
                to_right(me, ends, p).wait_send()

        @pl.when(me == n - 1)
        def _():
            for p in range(len(ends)):
                to_left(me, ends, p).wait_send()

    def wait_inner_sends():
        @pl.when(inner)
        def _():
            for j in range(n):
                pieces = ends if j in (0, n - 1) else middle
                for p in range(len(pieces)):
                    done = even & (p == marker)

                    @pl.when((j <= me) & ~(done & (far == 0) & (j == 1)))
                    def _():
                        to_right(j, pieces, p).wait_send()

                    @pl.when((j >= me) & ~(done & (far > 0) & (j == n - 2)))
                    def _():
                        to_left(j, pieces, p).wait_send()

    rotate_queries(0)
    pass_near(0)
    for b in range(1, batch):
        rotate_queries(b)
        if b < batch - 1:
            pass_near(b)
    for copy in own:
        copy.wait()
    for b in range(batch):
        prepare_entry(b, me)
    for b in range(batch - 1):
        prepare_near(b)
    for b in range(batch - 1):
        take_far(b)
    pass_near(batch - 1)
    prepare_near(batch - 1)
    wait_small_sends()
    wait_end_sends()
    take_far(batch - 1)
    wait_inner_sends()


def on_device(n, nf, q, k, v, bias, positions, rescale, table_index):
    batch, rows, width = q.shape
    heads_kv = k.shape[2] // HEAD_SIZE
    units = batch * heads_kv
    count = len(piece_list(batch, heads_kv, True))
    bias = bias.reshape(-1, HEAD_SIZE)
    hbm = pl.BlockSpec(memory_space=pltpu.HBM)
    dma = pltpu.SemaphoreType.DMA
    f32, bf16 = jnp.float32, jnp.bfloat16
    vmem = pl.BlockSpec(memory_space=pltpu.VMEM)
    heads_at_once = 8 if n <= 4 else 1
    results = pl.pallas_call(
        functools.partial(kernel, n, nf, heads_at_once),
        out_shape=[
            jax.ShapeDtypeStruct(q.shape, bf16),
            jax.ShapeDtypeStruct((units, GROUP * rows, HEAD_SIZE), bf16),
            jax.ShapeDtypeStruct((units, n, rows, HEAD_SIZE), bf16),
            jax.ShapeDtypeStruct((units, n, rows, HEAD_SIZE), bf16),
            jax.ShapeDtypeStruct((batch, rows, n * rows), f32),
        ],
        in_specs=[hbm] * 7,
        out_specs=[vmem] * 5,
        scratch_shapes=[
            pltpu.SMEM(table_index.shape, jnp.int32),
            pltpu.VMEM((n,) + positions.shape, jnp.int32),
            pltpu.VMEM(rescale.shape, f32),
            dma((4,)),
            pltpu.VMEM((batch, rows, width), bf16),
            pltpu.VMEM((n,) + k.shape, bf16),
            pltpu.VMEM((n,) + v.shape, bf16),
            pltpu.VMEM((batch, n, rows, HEAD_SIZE), f32),
            pltpu.VMEM((batch, n, rows, HEAD_SIZE), f32),
            pltpu.VMEM((nf,) + bias.shape, bf16),
            pltpu.VMEM((nf,) + bias.shape, f32),
            dma((batch,)), dma((2,)),
            dma((n, count)), dma((n, count)), dma((n, count)),
            dma((n,)), dma((n,)), dma((nf,)), dma((nf,)), dma((n,)), dma,
            pltpu.SemaphoreType.REGULAR((n,)), pltpu.SemaphoreType.REGULAR,
        ],
        compiler_params=pltpu.CompilerParams(
            collective_id=0, has_side_effects=True, vmem_limit_bytes=32 * 1024 * 1024
        ),
        name="relay_attention",
    )(*(pltpu.with_memory_space_constraint(x, pltpu.HBM) for x in (table_index, q, k, v, bias, positions, rescale)))
    return pl.pallas_call(
        functools.partial(write_kernel, heads_at_once),
        out_shape=jax.ShapeDtypeStruct(q.shape, bf16),
        in_specs=[vmem] * 5,
        out_specs=hbm,
        scratch_shapes=[pltpu.VMEM((rows, GROUP * HEAD_SIZE), bf16), dma((batch + 1,))],
        compiler_params=pltpu.CompilerParams(vmem_limit_bytes=24 * 1024 * 1024),
        name="write_result",
    )(*results)


def solution(mesh):
    in_specs = (
        P("fsdp", "ctx", "uly"),
        P("fsdp", "ctx", "uly"),
        P("fsdp", "ctx", "uly"),
        P("fsdp"),
        P("fsdp", "ctx"),
        P(),
        P("fsdp"),
    )
    n, nf = mesh.shape["ctx"], mesh.shape["fsdp"]
    return jax.shard_map(
        functools.partial(on_device, n, nf),
        mesh=mesh, in_specs=in_specs, out_specs=P("fsdp", "ctx", "uly"), check_vma=False,
    )
```

```python
import functools
import math

import jax
import jax.numpy as jnp
from jax import lax
from jax.experimental import pallas as pl
from jax.experimental.pallas import tpu as pltpu
from jax.sharding import PartitionSpec as P

QUERY_HEADS = 64
KEY_VALUE_HEADS = 8
HEAD_SIZE = 128
GROUP = QUERY_HEADS // KEY_VALUE_HEADS
RUN = 48

rope_base = 1000000.0
masked_value = -1e30
MESH = pl.DeviceIdType.MESH


def sine_cosine(angle):
    turns = jnp.floor(angle * (2.0 / math.pi) + 0.5)
    r = angle - turns * 1.5703125
    r = r - turns * 4.837512969970703125e-4
    r = r - turns * 7.54978995489188216e-8
    z = r * r
    s = r + r * z * (-1.6666654611e-1 + z * (8.3321608736e-3 - z * 1.9515295891e-4))
    c = 1.0 - 0.5 * z + z * z * (
        4.166664568298827e-2 + z * (-1.388731625493765e-3 + z * 2.443315711809948e-5)
    )
    quarter = turns.astype(jnp.int32) & 3
    odd = (quarter & 1) == 1
    sine = jnp.where(odd, c, s)
    cosine = jnp.where(odd, s, c)
    sine = jnp.where(quarter >= 2, -sine, sine)
    cosine = jnp.where((quarter == 1) | (quarter == 2), -cosine, cosine)
    return sine, cosine


def piece_list(batch, heads_kv, split_last):
    groups = [(b, 0, heads_kv) for b in range(batch)]
    if split_last:
        groups = groups[:-1] + [(batch - 1, g, 1) for g in range(heads_kv)]
    return groups


def attend_group(heads_at_once, q_ref, k_ref, v_ref, mask_ref, out_ref):
    shards, rows, _ = k_ref.shape
    keys = shards * rows
    scale = math.log2(math.e) / math.sqrt(HEAD_SIZE)
    k = k_ref[...].reshape(keys, HEAD_SIZE)
    v = v_ref[...].reshape(keys, HEAD_SIZE)
    mask = mask_ref[...]
    for i in range(0, GROUP, heads_at_once):
        q = q_ref[i * rows : (i + heads_at_once) * rows, :]
        s = lax.dot_general(
            q, k, (((1,), (1,)), ((), ())), preferred_element_type=jnp.float32
        )
        s = s.reshape(heads_at_once, rows, keys) + mask[None]
        high = jnp.max(s, axis=-1, keepdims=True)
        p = jnp.exp2((s - high) * scale)
        total = jnp.sum(p, axis=-1, keepdims=True)
        o = jnp.dot(
            p.astype(jnp.bfloat16).reshape(heads_at_once * rows, keys), v,
            preferred_element_type=jnp.float32,
        ).reshape(heads_at_once, rows, HEAD_SIZE)
        o = (o / total).astype(jnp.bfloat16)
        for e in range(heads_at_once):
            out_ref[:, (i + e) * HEAD_SIZE : (i + e + 1) * HEAD_SIZE] = o[e]


def write_kernel(heads_at_once, done_ref, q_ref, k_ref, v_ref, mask_ref, out_hbm, last, sems):
    batch = done_ref.shape[0]
    units, wide = q_ref.shape[0], last.shape[1]
    split = done_ref.shape[2] - wide
    copies = [
        pltpu.make_async_copy(done_ref.at[b], out_hbm.at[b], sems.at[b]) for b in range(batch - 1)
    ]
    if split:
        copies.append(pltpu.make_async_copy(
            done_ref.at[batch - 1, :, pl.ds(0, split)],
            out_hbm.at[batch - 1, :, pl.ds(0, split)], sems.at[batch - 1],
        ))
    for copy in copies:
        copy.start()
    u = units - 1
    attend_group(
        heads_at_once, q_ref.at[u], k_ref.at[u], v_ref.at[u], mask_ref.at[batch - 1], last
    )
    copy = pltpu.make_async_copy(
        last, out_hbm.at[batch - 1, :, pl.ds(split, wide)], sems.at[batch]
    )
    copy.start()
    for done in copies:
        done.wait()
    copy.wait()


def kernel(
    n, nf, heads_at_once,
    table_hbm, q_hbm, k_hbm, v_hbm, bias_hbm, pos_hbm, rescale_hbm,
    out_ref, q_rot, k_rot, v_all, mask_t,
    table_ref, pos_buf, rescale_ref, small_sem,
    q_buf, kv_buf, cos_t, sin_t, bias_buf, bias_f,
    q_sem, own_sem, send_right, send_left, recv_sem,
    pos_send, pos_recv, bias_send, bias_recv, spread_send, spread_recv, ready, turn,
):
    batch, rows, _ = q_hbm.shape
    heads_kv = k_hbm.shape[2] // HEAD_SIZE
    units = batch * heads_kv
    me = lax.axis_index("ctx")
    mf = lax.axis_index("fsdp")
    mu = lax.axis_index("uly")
    shard_rows = bias_hbm.shape[0]
    ends = piece_list(batch, heads_kv, True)
    middle = piece_list(batch, heads_kv, False)
    wide = GROUP * HEAD_SIZE
    far = jnp.where(2 * me <= n - 1, n - 1, 0)

    barrier = pltpu.get_barrier_semaphore()

    inner = (me > 0) & (me < n - 1)
    even = mf % 2 == 0

    @pl.when(inner & ~even)
    def _():
        pl.semaphore_signal(barrier, inc=1, device_id={"fsdp": mf - 1}, device_id_type=MESH)

    @pl.when(inner & even)
    def _():
        pl.semaphore_wait(barrier, 2)

    @pl.when((inner & ~even) | (me == n - 1))
    def _():
        pl.semaphore_wait(barrier, 1)

    @pl.when(me < n - 1)
    def _():
        pl.semaphore_signal(barrier, inc=1, device_id={"ctx": me + 1}, device_id_type=MESH)

    @pl.when(me == 0)
    def _():
        for d in range(1, nf):
            pl.semaphore_signal(
                barrier, inc=1, device_id={"fsdp": lax.rem(mf + d, nf)}, device_id_type=MESH
            )
        pl.semaphore_wait(barrier, nf - 1)

    def pos_copy(source, target):
        return pltpu.make_async_remote_copy(
            src_ref=pos_hbm, dst_ref=pos_buf.at[source],
            send_sem=pos_send.at[target], recv_sem=pos_recv.at[source],
            device_id={"ctx": target}, device_id_type=MESH,
        )

    def remote(shard, pieces, p, sems, target, source=None, kind=slice(None)):
        b, g, heads = pieces[p]
        lanes = pl.ds(g * HEAD_SIZE, heads * HEAD_SIZE)
        place = kv_buf.at[shard, b, kind, :, lanes]
        return pltpu.make_async_remote_copy(
            src_ref=place if source is None else source.at[b, :, lanes], dst_ref=place,
            send_sem=sems.at[shard, p], recv_sem=recv_sem.at[shard, p],
            device_id={"ctx": target}, device_id_type=MESH,
        )

    def to_right(shard, pieces, p, *own):
        return remote(shard, pieces, p, send_right, lax.rem(me + 1, n), *own)

    def to_left(shard, pieces, p, *own):
        return remote(shard, pieces, p, send_left, lax.rem(me + n - 1, n), *own)

    def start_own(to_side, pieces, first=0, last=None):
        for p in range(len(pieces))[first:last]:
            for kind, source in enumerate((k_hbm, v_hbm)):
                to_side(me, pieces, p, source, kind).start()

    def say_ready():
        for j in range(n - 2, -1, -1):
            @pl.when(j < me)
            def _():
                pl.semaphore_signal(
                    ready.at[me], inc=1, device_id={"ctx": j}, device_id_type=MESH
                )

        for j in range(n - 1):
            @pl.when(j < me)
            def _():
                pos_copy(me, j).start()

    @pl.when(me == n - 1)
    def _():
        say_ready()
        start_own(to_left, ends)

    @pl.when(inner)
    def _():
        start_own(to_left, middle, 0, 1)
        say_ready()
        start_own(to_left, middle, 1, None)

    small = [
        pltpu.make_async_copy(source, target, small_sem.at[i])
        for i, (source, target) in enumerate(
            (
                (pos_hbm, pos_buf.at[me]), (rescale_hbm, rescale_ref),
                (table_hbm, table_ref),
            )
        )
    ]
    own_bias = pltpu.make_async_copy(bias_hbm, bias_buf.at[mf], small_sem.at[3])
    for copy in small:
        copy.start()

    @pl.when(me == 0)
    def _():
        own_bias.start()

    def q_copy(b):
        return pltpu.make_async_copy(q_hbm.at[b], q_buf.at[b], q_sem.at[b])

    own = (
        pltpu.make_async_copy(k_hbm, kv_buf.at[me, :, 0], own_sem.at[0]),
        pltpu.make_async_copy(v_hbm, kv_buf.at[me, :, 1], own_sem.at[1]),
    )

    for copy in own:
        copy.start()
    def bias_copy(source, target):
        return pltpu.make_async_remote_copy(
            src_ref=bias_hbm, dst_ref=bias_buf.at[source],
            send_sem=bias_send.at[target], recv_sem=bias_recv.at[source],
            device_id={"fsdp": target}, device_id_type=MESH,
        )

    def spread_copy(target):
        return pltpu.make_async_remote_copy(
            src_ref=bias_buf, dst_ref=bias_buf,
            send_sem=spread_send.at[target], recv_sem=spread_recv,
            device_id={"ctx": target}, device_id_type=MESH,
        )

    @pl.when(me == 0)
    def _():
        for d in range(1, nf):
            bias_copy(mf, lax.rem(mf + d, nf)).start()
        own_bias.wait()
        for d in range(1, nf):
            other = lax.rem(mf + d, nf)
            bias_copy(other, other).wait_recv()

    for j in range(1, n):
        @pl.when(me < j)
        def _():
            pl.semaphore_wait(ready.at[j], 1)
            pos_copy(me, j).start()

        @pl.when((me < j) & (me == 0))
        def _():
            spread_copy(j).start()

    @pl.when(me == 0)
    def _():
        start_own(to_right, ends)

    @pl.when(inner)
    def _():
        start_own(to_right, middle)

    for b in range(batch):
        q_copy(b).start()
    for copy in small:
        copy.wait()

    @pl.when(me > 0)
    def _():
        spread_copy(0).wait_recv()

    for f in range(nf):
        bias_f[f] = bias_buf[f].astype(jnp.float32)

    def bias_row(row):
        return bias_f[row // shard_rows, pl.ds(row % shard_rows, 1), :]

    for j in range(n):
        @pl.when(j != me)
        def _():
            pos_copy(j, j).wait_recv()

    lane = lax.broadcasted_iota(jnp.int32, (1, HEAD_SIZE), 1)
    power = jnp.exp(
        (lane % (HEAD_SIZE // 2)).astype(jnp.float32)
        * (2.0 / HEAD_SIZE * math.log(rope_base))
    )
    low_half = lane < HEAD_SIZE // 2
    run_rows = lax.broadcasted_iota(jnp.int32, (RUN, HEAD_SIZE), 0)
    query_row = lax.broadcasted_iota(jnp.int32, (RUN, 1), 0)
    keys = n * rows
    key_lane = lax.broadcasted_iota(jnp.int32, (1, keys), 1)

    for b in range(batch):
        factors = rescale_ref[0:1, :]
        for t in range(1, rescale_ref.shape[0]):
            factors = jnp.where(table_ref[b] == t, rescale_ref[t : t + 1, :], factors)
        inverse = 1.0 / (jnp.concatenate([factors, factors], axis=1) * power)
        key_pos = key_lane % RUN
        for j in range(n):
            for piece in range(rows // RUN):
                first = pos_buf[j, b : b + 1, piece * RUN : piece * RUN + 1]
                here = key_lane // RUN == j * (rows // RUN) + piece
                key_pos = key_pos + jnp.where(here, first, 0)
                place = (run_rows + first).astype(jnp.float32)
                sine, cosine = sine_cosine(place * inverse)
                block = slice(piece * RUN, (piece + 1) * RUN)
                cos_t[b, j, block, :] = cosine
                sin_t[b, j, block, :] = jnp.where(low_half, -sine, sine)
        for piece in range(rows // RUN):
            first = pos_buf[me, b : b + 1, piece * RUN : piece * RUN + 1]
            mask_t[b, piece * RUN : (piece + 1) * RUN, :] = jnp.where(
                key_pos <= query_row + first, 0.0, masked_value
            )

    def rotate(x, cosine, sine):
        return x * cosine + pltpu.roll(x, HEAD_SIZE // 2, 1) * sine

    query_heads_here = heads_kv * GROUP

    def rotate_queries(b):
        q_copy(b).wait()

        @pl.loop(0, heads_kv)
        def _(g):
            for i in range(GROUP):
                x = q_buf[
                    b, :, pl.ds(pl.multiple_of(g * wide + i * HEAD_SIZE, HEAD_SIZE), HEAD_SIZE)
                ].astype(jnp.float32)
                x = x + bias_row(mu * query_heads_here + g * GROUP + i)
                q_rot[b * heads_kv + g, i * rows : (i + 1) * rows, :] = rotate(
                    x, cos_t[b, me], sin_t[b, me]
                ).astype(jnp.bfloat16)

    def prepare(u, j):
        b, g = u // heads_kv, u % heads_kv
        lanes = pl.ds(pl.multiple_of(g * HEAD_SIZE, HEAD_SIZE), HEAD_SIZE)
        x = kv_buf[j, b, 0, :, lanes].astype(jnp.float32)
        x = x + bias_row(QUERY_HEADS + mu * heads_kv + g)
        k_rot[u, j] = rotate(x, cos_t[b, j], sin_t[b, j]).astype(jnp.bfloat16)
        x = kv_buf[j, b, 1, :, lanes].astype(jnp.float32)
        x = x + bias_row(QUERY_HEADS + KEY_VALUE_HEADS + mu * heads_kv + g)
        v_all[u, j] = x.astype(jnp.bfloat16)

    def attend(u):
        b, g = u // heads_kv, u % heads_kv
        attend_group(
            heads_at_once, q_rot.at[u], k_rot.at[u], v_all.at[u], mask_t.at[b],
            out_ref.at[b, :, pl.ds(pl.multiple_of(g * wide, wide), wide)],
        )

    def pass_left(shard, pieces, p):
        to_left(shard, pieces, p).wait_recv()

        @pl.when(me > 0)
        def _():
            to_left(shard, pieces, p).start()

    def pass_right(shard, pieces, p):
        to_right(shard, pieces, p).wait_recv()

        @pl.when(me < n - 1)
        def _():
            to_right(shard, pieces, p).start()

    def of_entry(pieces, b):
        return [p for p, piece in enumerate(pieces) if piece[0] == b]

    def prepare_entry(b, j):
        @pl.loop(b * heads_kv, (b + 1) * heads_kv)
        def _(u):
            prepare(u, j)

    def each_near(act):
        for hop in range(1, n):
            right, left = me + hop, me - hop

            @pl.when((right < n) & (right != far))
            def _():
                act(right, pass_left, right == n - 1)

            @pl.when((left >= 0) & (left != far))
            def _():
                act(left, pass_right, left == 0)

    def pass_near(b):
        def act(shard, hand_on, at_end):
            for pieces, chosen in ((ends, at_end), (middle, ~at_end)):
                @pl.when(chosen)
                def _():
                    for p in of_entry(pieces, b):
                        hand_on(shard, pieces, p)

        each_near(act)

    def prepare_near(b):
        each_near(lambda shard, hand_on, at_end: prepare_entry(b, shard))

    def pass_far(p):
        to_left(far, ends, p).wait_recv()

        @pl.when(inner & (far > 0))
        def _():
            to_left(far, ends, p).start()

        @pl.when(inner & (far == 0))
        def _():
            to_right(far, ends, p).start()

    marker = of_entry(middle, 0)[-1]

    def hold_odd():
        @pl.when(inner & ~even)
        def _():
            pl.semaphore_wait(turn, 1)

    def release_odd():
        @pl.when(inner & even)
        def _():
            @pl.when(far > 0)
            def _():
                to_left(n - 2, middle, marker).wait_send()

            @pl.when(far == 0)
            def _():
                to_right(1, middle, marker).wait_send()

            pl.semaphore_signal(turn, inc=1, device_id={"fsdp": mf + 1}, device_id_type=MESH)

    def take_far(b):
        steps = {}
        for p in of_entry(ends, b):
            steps.setdefault(ends[p][1], []).append(p)
        starts = sorted(steps) + [heads_kv]
        for first, last in zip(starts, starts[1:]):
            for p in steps[first]:
                pass_far(p)
            if last - first > 1:
                @pl.loop(b * heads_kv + first, b * heads_kv + last)
                def _(u):
                    prepare(u, far)
                    attend(u)
            else:
                prepare(b * heads_kv + first, far)
                if b * heads_kv + last < units:
                    attend(b * heads_kv + first)

    def wait_small_sends():
        for j in range(n):
            @pl.when(j != me)
            def _():
                pos_copy(me, j).wait_send()

        @pl.when(me == 0)
        def _():
            for d in range(1, nf):
                bias_copy(mf, lax.rem(mf + d, nf)).wait_send()
            for j in range(1, n):
                spread_copy(j).wait_send()

    def wait_end_sends():
        @pl.when(me == 0)
        def _():
            for p in range(len(ends)):
                to_right(me, ends, p).wait_send()

        @pl.when(me == n - 1)
        def _():
            for p in range(len(ends)):
                to_left(me, ends, p).wait_send()

    def wait_inner_sends():
        @pl.when(inner)
        def _():
            for j in range(n):
                pieces = ends if j in (0, n - 1) else middle
                for p in range(len(pieces)):
                    done = even & (p == marker)

                    @pl.when((j <= me) & ~(done & (far == 0) & (j == 1)))
                    def _():
                        to_right(j, pieces, p).wait_send()

                    @pl.when((j >= me) & ~(done & (far > 0) & (j == n - 2)))
                    def _():
                        to_left(j, pieces, p).wait_send()

    rotate_queries(0)
    pass_near(0)
    for b in range(1, batch):
        rotate_queries(b)
    for copy in own:
        copy.wait()
    for b in range(batch):
        prepare_entry(b, me)
    prepare_near(0)
    for b in range(1, batch - 1):
        if b == 1:
            hold_odd()
        pass_near(b)
        if b == 1:
            release_odd()
        prepare_near(b)
    for b in range(batch - 1):
        take_far(b)
    pass_near(batch - 1)
    prepare_near(batch - 1)
    wait_small_sends()
    wait_end_sends()
    take_far(batch - 1)
    wait_inner_sends()


def on_device(n, nf, q, k, v, bias, positions, rescale, table_index):
    batch, rows, width = q.shape
    heads_kv = k.shape[2] // HEAD_SIZE
    units = batch * heads_kv
    count = len(piece_list(batch, heads_kv, True))
    bias = bias.reshape(-1, HEAD_SIZE)
    hbm = pl.BlockSpec(memory_space=pltpu.HBM)
    dma = pltpu.SemaphoreType.DMA
    f32, bf16 = jnp.float32, jnp.bfloat16
    vmem = pl.BlockSpec(memory_space=pltpu.VMEM)
    heads_at_once = 8 if n <= 4 else 1
    results = pl.pallas_call(
        functools.partial(kernel, n, nf, heads_at_once),
        out_shape=[
            jax.ShapeDtypeStruct(q.shape, bf16),
            jax.ShapeDtypeStruct((units, GROUP * rows, HEAD_SIZE), bf16),
            jax.ShapeDtypeStruct((units, n, rows, HEAD_SIZE), bf16),
            jax.ShapeDtypeStruct((units, n, rows, HEAD_SIZE), bf16),
            jax.ShapeDtypeStruct((batch, rows, n * rows), f32),
        ],
        in_specs=[hbm] * 7,
        out_specs=[vmem] * 5,
        scratch_shapes=[
            pltpu.SMEM(table_index.shape, jnp.int32),
            pltpu.VMEM((n,) + positions.shape, jnp.int32),
            pltpu.VMEM(rescale.shape, f32),
            dma((4,)),
            pltpu.VMEM((batch, rows, width), bf16),
            pltpu.VMEM((n, batch, 2) + k.shape[1:], bf16),
            pltpu.VMEM((batch, n, rows, HEAD_SIZE), f32),
            pltpu.VMEM((batch, n, rows, HEAD_SIZE), f32),
            pltpu.VMEM((nf,) + bias.shape, bf16),
            pltpu.VMEM((nf,) + bias.shape, f32),
            dma((batch,)), dma((2,)),
            dma((n, count)), dma((n, count)), dma((n, count)),
            dma((n,)), dma((n,)), dma((nf,)), dma((nf,)), dma((n,)), dma,
            pltpu.SemaphoreType.REGULAR((n,)), pltpu.SemaphoreType.REGULAR,
        ],
        compiler_params=pltpu.CompilerParams(
            collective_id=0, has_side_effects=True, vmem_limit_bytes=32 * 1024 * 1024
        ),
        name="relay_attention",
    )(*(pltpu.with_memory_space_constraint(x, pltpu.HBM) for x in (table_index, q, k, v, bias, positions, rescale)))
    return pl.pallas_call(
        functools.partial(write_kernel, heads_at_once),
        out_shape=jax.ShapeDtypeStruct(q.shape, bf16),
        in_specs=[vmem] * 5,
        out_specs=hbm,
        scratch_shapes=[pltpu.VMEM((rows, GROUP * HEAD_SIZE), bf16), dma((batch + 1,))],
        compiler_params=pltpu.CompilerParams(vmem_limit_bytes=24 * 1024 * 1024),
        name="write_result",
    )(*results)


def solution(mesh):
    in_specs = (
        P("fsdp", "ctx", "uly"),
        P("fsdp", "ctx", "uly"),
        P("fsdp", "ctx", "uly"),
        P("fsdp"),
        P("fsdp", "ctx"),
        P(),
        P("fsdp"),
    )
    n, nf = mesh.shape["ctx"], mesh.shape["fsdp"]
    return jax.shard_map(
        functools.partial(on_device, n, nf),
        mesh=mesh, in_specs=in_specs, out_specs=P("fsdp", "ctx", "uly"), check_vma=False,
    )
```

```python
import functools
import math

import jax
import jax.numpy as jnp
from jax import lax
from jax.experimental import pallas as pl
from jax.experimental.pallas import tpu as pltpu
from jax.sharding import PartitionSpec as P

QUERY_HEADS = 64
KEY_VALUE_HEADS = 8
HEAD_SIZE = 128
GROUP = QUERY_HEADS // KEY_VALUE_HEADS
RUN = 48
LATE_KEYS = 128
EARLY_GROUPS = 2

rope_base = 1000000.0
masked_value = -1e30
MESH = pl.DeviceIdType.MESH


def sine_cosine(angle):
    turns = jnp.floor(angle * (2.0 / math.pi) + 0.5)
    r = angle - turns * 1.5703125
    r = r - turns * 4.837512969970703125e-4
    r = r - turns * 7.54978995489188216e-8
    z = r * r
    s = r + r * z * (-1.6666654611e-1 + z * (8.3321608736e-3 - z * 1.9515295891e-4))
    c = 1.0 - 0.5 * z + z * z * (
        4.166664568298827e-2 + z * (-1.388731625493765e-3 + z * 2.443315711809948e-5)
    )
    quarter = turns.astype(jnp.int32) & 3
    odd = (quarter & 1) == 1
    sine = jnp.where(odd, c, s)
    cosine = jnp.where(odd, s, c)
    sine = jnp.where(quarter >= 2, -sine, sine)
    cosine = jnp.where((quarter == 1) | (quarter == 2), -cosine, cosine)
    return sine, cosine


def piece_list(batch, heads_kv, split_last):
    groups = [(b, 0, heads_kv) for b in range(batch)]
    if split_last:
        groups = groups[:-1] + [(batch - 1, g, 1) for g in range(heads_kv)]
    return groups


def group_scores(q_ref, k_ref, mask_ref, first, count, columns):
    shards, rows, _ = k_ref.shape
    s = lax.dot_general(
        q_ref[first * rows : (first + count) * rows, :],
        k_ref[...].reshape(shards * rows, HEAD_SIZE)[columns],
        (((1,), (1,)), ((), ())), preferred_element_type=jnp.float32,
    )
    wide = s.shape[1]
    s = s.reshape(count, rows, wide) + mask_ref[...][None, :, columns]
    return s.reshape(count * rows, wide)


def group_blend(p, v_ref, columns):
    shards, rows, _ = v_ref.shape
    return jnp.dot(
        p.astype(jnp.bfloat16), v_ref[...].reshape(shards * rows, HEAD_SIZE)[columns],
        preferred_element_type=jnp.float32,
    )


def store_heads(out_ref, o, first, count):
    rows = out_ref.shape[0]
    o = o.astype(jnp.bfloat16)
    for e in range(count):
        lanes = slice((first + e) * HEAD_SIZE, (first + e + 1) * HEAD_SIZE)
        out_ref[:, lanes] = o[e * rows : (e + 1) * rows]


SCALE = math.log2(math.e) / math.sqrt(HEAD_SIZE)


def attend_group(count, q_ref, k_ref, v_ref, mask_ref, out_ref):
    columns = slice(None)
    for i in range(0, GROUP, count):
        s = group_scores(q_ref, k_ref, mask_ref, i, count, columns)
        high = jnp.max(s, axis=-1, keepdims=True)
        p = jnp.exp2((s - high) * SCALE)
        total = jnp.sum(p, axis=-1, keepdims=True)
        store_heads(out_ref, group_blend(p, v_ref, columns) / total, i, count)


def attend_early(count, q_ref, k_ref, v_ref, mask_ref, part_ref, log_ref):
    rows = k_ref.shape[1]
    columns = slice(LATE_KEYS, None)
    for i in range(0, GROUP, count):
        at = slice(i * rows, (i + count) * rows)
        s = group_scores(q_ref, k_ref, mask_ref, i, count, columns)
        high = jnp.max(s, axis=-1, keepdims=True)
        p = jnp.exp2((s - high) * SCALE)
        total = jnp.sum(p, axis=-1, keepdims=True)
        part_ref[at, :] = group_blend(p, v_ref, columns) / total
        log_ref[at, :] = jnp.broadcast_to(
            high + jnp.log2(total) * (1.0 / SCALE), (count * rows, HEAD_SIZE)
        )


def attend_late(count, q_ref, k_ref, v_ref, mask_ref, part_ref, log_ref, out_ref):
    rows = k_ref.shape[1]
    columns = slice(0, LATE_KEYS)
    for i in range(0, GROUP, count):
        at = slice(i * rows, (i + count) * rows)
        s = group_scores(q_ref, k_ref, mask_ref, i, count, columns)
        before = log_ref[at, :]
        high = jnp.maximum(before, jnp.max(s, axis=-1, keepdims=True))
        p = jnp.exp2((s - high) * SCALE)
        keep = jnp.exp2((before - high) * SCALE)
        total = keep + jnp.sum(p, axis=-1, keepdims=True)
        o = (part_ref[at, :] * keep + group_blend(p, v_ref, columns)) / total
        store_heads(out_ref, o, i, count)


def write_kernel(
    heads_at_once, done_ref, q_ref, k_ref, v_ref, mask_ref, part_ref, log_ref,
    out_hbm, last, sems,
):
    batch = done_ref.shape[0]
    units, wide = q_ref.shape[0], last.shape[1]
    split = done_ref.shape[2] - wide
    copies = [
        pltpu.make_async_copy(done_ref.at[b], out_hbm.at[b], sems.at[b]) for b in range(batch - 1)
    ]
    if split:
        copies.append(pltpu.make_async_copy(
            done_ref.at[batch - 1, :, pl.ds(0, split)],
            out_hbm.at[batch - 1, :, pl.ds(0, split)], sems.at[batch - 1],
        ))
    for copy in copies:
        copy.start()
    u = units - 1
    e = part_ref.shape[0] - 1
    attend_late(
        heads_at_once, q_ref.at[u], k_ref.at[u], v_ref.at[u], mask_ref.at[batch - 1],
        part_ref.at[e], log_ref.at[e], last,
    )
    copy = pltpu.make_async_copy(
        last, out_hbm.at[batch - 1, :, pl.ds(split, wide)], sems.at[batch]
    )
    copy.start()
    for done in copies:
        done.wait()
    copy.wait()


def kernel(
    n, nf, heads_at_once,
    table_hbm, q_hbm, k_hbm, v_hbm, bias_hbm, pos_hbm, rescale_hbm,
    out_ref, q_rot, k_rot, v_all, mask_t, early, early_log,
    table_ref, pos_buf, rescale_ref, small_sem,
    q_buf, kv_buf, cos_t, sin_t, bias_buf, bias_f,
    q_sem, own_sem, send_right, send_left, recv_sem,
    pos_send, pos_recv, bias_send, bias_recv, spread_send, spread_recv, ready, turn,
):
    batch, rows, _ = q_hbm.shape
    heads_kv = k_hbm.shape[2] // HEAD_SIZE
    units = batch * heads_kv
    me = lax.axis_index("ctx")
    mf = lax.axis_index("fsdp")
    mu = lax.axis_index("uly")
    shard_rows = bias_hbm.shape[0]
    ends = piece_list(batch, heads_kv, True)
    middle = piece_list(batch, heads_kv, False)
    wide = GROUP * HEAD_SIZE
    far = jnp.where(2 * me <= n - 1, n - 1, 0)

    def slot_of(j):
        return jnp.where(far > 0, far - j, j)


    barrier = pltpu.get_barrier_semaphore()

    inner = (me > 0) & (me < n - 1)
    even = mf % 2 == 0

    @pl.when(inner & ~even)
    def _():
        pl.semaphore_signal(barrier, inc=1, device_id={"fsdp": mf - 1}, device_id_type=MESH)

    @pl.when(inner & even)
    def _():
        pl.semaphore_wait(barrier, 2)

    @pl.when((inner & ~even) | (me == n - 1))
    def _():
        pl.semaphore_wait(barrier, 1)

    @pl.when(me < n - 1)
    def _():
        pl.semaphore_signal(barrier, inc=1, device_id={"ctx": me + 1}, device_id_type=MESH)

    @pl.when(me == 0)
    def _():
        for d in range(1, nf):
            pl.semaphore_signal(
                barrier, inc=1, device_id={"fsdp": lax.rem(mf + d, nf)}, device_id_type=MESH
            )
        pl.semaphore_wait(barrier, nf - 1)

    def pos_copy(source, target):
        return pltpu.make_async_remote_copy(
            src_ref=pos_hbm, dst_ref=pos_buf.at[source],
            send_sem=pos_send.at[target], recv_sem=pos_recv.at[source],
            device_id={"ctx": target}, device_id_type=MESH,
        )

    def remote(shard, pieces, p, sems, target, source=None, kind=slice(None)):
        b, g, heads = pieces[p]
        lanes = pl.ds(g * HEAD_SIZE, heads * HEAD_SIZE)
        place = kv_buf.at[shard, b, kind, :, lanes]
        return pltpu.make_async_remote_copy(
            src_ref=place if source is None else source.at[b, :, lanes], dst_ref=place,
            send_sem=sems.at[shard, p], recv_sem=recv_sem.at[shard, p],
            device_id={"ctx": target}, device_id_type=MESH,
        )

    def to_right(shard, pieces, p, *own):
        return remote(shard, pieces, p, send_right, lax.rem(me + 1, n), *own)

    def to_left(shard, pieces, p, *own):
        return remote(shard, pieces, p, send_left, lax.rem(me + n - 1, n), *own)

    def start_own(to_side, pieces, first=0, last=None):
        for p in range(len(pieces))[first:last]:
            for kind, source in enumerate((k_hbm, v_hbm)):
                to_side(me, pieces, p, source, kind).start()

    def say_ready():
        for j in range(n - 2, -1, -1):
            @pl.when(j < me)
            def _():
                pl.semaphore_signal(
                    ready.at[me], inc=1, device_id={"ctx": j}, device_id_type=MESH
                )

        for j in range(n - 1):
            @pl.when(j < me)
            def _():
                pos_copy(me, j).start()

    @pl.when(me == n - 1)
    def _():
        say_ready()
        start_own(to_left, ends)

    @pl.when(inner)
    def _():
        start_own(to_left, middle, 0, 1)
        say_ready()
        start_own(to_left, middle, 1, None)

    small = [
        pltpu.make_async_copy(source, target, small_sem.at[i])
        for i, (source, target) in enumerate(
            (
                (pos_hbm, pos_buf.at[me]), (rescale_hbm, rescale_ref),
                (table_hbm, table_ref),
            )
        )
    ]
    own_bias = pltpu.make_async_copy(bias_hbm, bias_buf.at[mf], small_sem.at[3])
    for copy in small:
        copy.start()

    @pl.when(me == 0)
    def _():
        own_bias.start()

    def q_copy(b):
        return pltpu.make_async_copy(q_hbm.at[b], q_buf.at[b], q_sem.at[b])

    own = (
        pltpu.make_async_copy(k_hbm, kv_buf.at[me, :, 0], own_sem.at[0]),
        pltpu.make_async_copy(v_hbm, kv_buf.at[me, :, 1], own_sem.at[1]),
    )

    def bias_copy(source, target):
        return pltpu.make_async_remote_copy(
            src_ref=bias_hbm, dst_ref=bias_buf.at[source],
            send_sem=bias_send.at[target], recv_sem=bias_recv.at[source],
            device_id={"fsdp": target}, device_id_type=MESH,
        )

    def spread_copy(target):
        return pltpu.make_async_remote_copy(
            src_ref=bias_buf, dst_ref=bias_buf,
            send_sem=spread_send.at[target], recv_sem=spread_recv,
            device_id={"ctx": target}, device_id_type=MESH,
        )

    @pl.when(me == 0)
    def _():
        for d in range(1, nf):
            bias_copy(mf, lax.rem(mf + d, nf)).start()
        own_bias.wait()
        for d in range(1, nf):
            other = lax.rem(mf + d, nf)
            bias_copy(other, other).wait_recv()

    for j in range(1, n):
        @pl.when(me < j)
        def _():
            pl.semaphore_wait(ready.at[j], 1)

            if j == n - 1:
                @pl.when(me == n - 2)
                def _():
                    start_own(to_right, middle, 0, 1)

            pos_copy(me, j).start()

        @pl.when((me < j) & (me == 0))
        def _():
            spread_copy(j).start()

    @pl.when(me == 0)
    def _():
        start_own(to_right, ends)

    @pl.when(inner & (me < n - 2))
    def _():
        start_own(to_right, middle)

    @pl.when(me == n - 2)
    def _():
        start_own(to_right, middle, 1, None)

    for copy in own:
        copy.start()
    for b in range(batch):
        q_copy(b).start()
    for copy in small:
        copy.wait()

    @pl.when(me > 0)
    def _():
        spread_copy(0).wait_recv()

    for f in range(nf):
        bias_f[f] = bias_buf[f].astype(jnp.float32)

    def bias_row(row):
        return bias_f[row // shard_rows, pl.ds(row % shard_rows, 1), :]

    for j in range(n):
        @pl.when(j != me)
        def _():
            pos_copy(j, j).wait_recv()

    lane = lax.broadcasted_iota(jnp.int32, (1, HEAD_SIZE), 1)
    power = jnp.exp(
        (lane % (HEAD_SIZE // 2)).astype(jnp.float32)
        * (2.0 / HEAD_SIZE * math.log(rope_base))
    )
    low_half = lane < HEAD_SIZE // 2
    run_rows = lax.broadcasted_iota(jnp.int32, (RUN, HEAD_SIZE), 0)
    query_row = lax.broadcasted_iota(jnp.int32, (RUN, 1), 0)
    keys = n * rows
    key_lane = lax.broadcasted_iota(jnp.int32, (1, keys), 1)

    for b in range(batch):
        factors = rescale_ref[0:1, :]
        for t in range(1, rescale_ref.shape[0]):
            factors = jnp.where(table_ref[b] == t, rescale_ref[t : t + 1, :], factors)
        inverse = 1.0 / (jnp.concatenate([factors, factors], axis=1) * power)
        key_pos = key_lane % RUN
        for j in range(n):
            for piece in range(rows // RUN):
                first = pos_buf[j, b : b + 1, piece * RUN : piece * RUN + 1]
                here = key_lane // RUN == slot_of(j) * (rows // RUN) + piece
                key_pos = key_pos + jnp.where(here, first, 0)
                place = (run_rows + first).astype(jnp.float32)
                sine, cosine = sine_cosine(place * inverse)
                block = slice(piece * RUN, (piece + 1) * RUN)
                cos_t[b, j, block, :] = cosine
                sin_t[b, j, block, :] = jnp.where(low_half, -sine, sine)
        for piece in range(rows // RUN):
            first = pos_buf[me, b : b + 1, piece * RUN : piece * RUN + 1]
            mask_t[b, piece * RUN : (piece + 1) * RUN, :] = jnp.where(
                key_pos <= query_row + first, 0.0, masked_value
            )

    def rotate(x, cosine, sine):
        return x * cosine + pltpu.roll(x, HEAD_SIZE // 2, 1) * sine

    query_heads_here = heads_kv * GROUP

    def rotate_queries(b):
        q_copy(b).wait()

        @pl.loop(0, heads_kv)
        def _(g):
            for i in range(GROUP):
                x = q_buf[
                    b, :, pl.ds(pl.multiple_of(g * wide + i * HEAD_SIZE, HEAD_SIZE), HEAD_SIZE)
                ].astype(jnp.float32)
                x = x + bias_row(mu * query_heads_here + g * GROUP + i)
                q_rot[b * heads_kv + g, i * rows : (i + 1) * rows, :] = rotate(
                    x, cos_t[b, me], sin_t[b, me]
                ).astype(jnp.bfloat16)

    def prepare(u, j):
        b, g = u // heads_kv, u % heads_kv
        slot = slot_of(j)
        lanes = pl.ds(pl.multiple_of(g * HEAD_SIZE, HEAD_SIZE), HEAD_SIZE)
        x = kv_buf[j, b, 0, :, lanes].astype(jnp.float32)
        x = x + bias_row(QUERY_HEADS + mu * heads_kv + g)
        k_rot[u, slot] = rotate(x, cos_t[b, j], sin_t[b, j]).astype(jnp.bfloat16)
        x = kv_buf[j, b, 1, :, lanes].astype(jnp.float32)
        x = x + bias_row(QUERY_HEADS + KEY_VALUE_HEADS + mu * heads_kv + g)
        v_all[u, slot] = x.astype(jnp.bfloat16)

    def group_refs(u):
        return q_rot.at[u], k_rot.at[u], v_all.at[u], mask_t.at[u // heads_kv]

    def out_of(u):
        g = u % heads_kv
        return out_ref.at[u // heads_kv, :, pl.ds(pl.multiple_of(g * wide, wide), wide)]

    first_early = units - early.shape[0]

    def attend(u):
        attend_group(heads_at_once, *group_refs(u), out_of(u))

    def pass_left(shard, pieces, p):
        to_left(shard, pieces, p).wait_recv()

        @pl.when(me > 0)
        def _():
            to_left(shard, pieces, p).start()

    def pass_right(shard, pieces, p):
        to_right(shard, pieces, p).wait_recv()

        @pl.when(me < n - 1)
        def _():
            to_right(shard, pieces, p).start()

    def of_entry(pieces, b):
        return [p for p, piece in enumerate(pieces) if piece[0] == b]

    def prepare_entry(b, j):
        @pl.loop(b * heads_kv, (b + 1) * heads_kv)
        def _(u):
            prepare(u, j)

    def each_near(act, hops=range(1, n)):
        for hop in hops:
            right, left = me + hop, me - hop

            @pl.when((right < n) & (right != far))
            def _():
                act(right, pass_left, right == n - 1)

            @pl.when((left >= 0) & (left != far))
            def _():
                act(left, pass_right, left == 0)

    def pass_near(b, *hops):
        def act(shard, hand_on, at_end):
            for pieces, chosen in ((ends, at_end), (middle, ~at_end)):
                @pl.when(chosen)
                def _():
                    for p in of_entry(pieces, b):
                        hand_on(shard, pieces, p)

        each_near(act, *hops)

    def prepare_near(b, *hops):
        each_near(lambda shard, hand_on, at_end: prepare_entry(b, shard), *hops)

    def pass_far(p):
        to_left(far, ends, p).wait_recv()

        @pl.when(inner & (far > 0))
        def _():
            to_left(far, ends, p).start()

        @pl.when(inner & (far == 0))
        def _():
            to_right(far, ends, p).start()

    marker = of_entry(middle, 0)[-1]

    def hold_odd():
        @pl.when(inner & ~even)
        def _():
            pl.semaphore_wait(turn, 1)

    def release_odd():
        @pl.when(inner & even)
        def _():
            @pl.when(far > 0)
            def _():
                to_left(n - 2, middle, marker).wait_send()

            @pl.when(far == 0)
            def _():
                to_right(1, middle, marker).wait_send()

            pl.semaphore_signal(turn, inc=1, device_id={"fsdp": mf + 1}, device_id_type=MESH)

    def take_far(b):
        if b == batch - 1:
            @pl.when(inner)
            def _():
                for p in of_entry(ends, b):
                    pass_far(p)
        steps = {}
        for p in of_entry(ends, b):
            steps.setdefault(ends[p][1], []).append(p)
        starts = sorted(steps) + [heads_kv]
        for first, last in zip(starts, starts[1:]):
            for p in steps[first]:
                if b < batch - 1:
                    pass_far(p)
                else:
                    @pl.when(~inner)
                    def _():
                        to_left(far, ends, p).wait_recv()
            if b == batch - 2:
                @pl.when(inner)
                def _():
                    pass_near(batch - 1)
            if last - first > 1:
                @pl.loop(b * heads_kv + first, b * heads_kv + last)
                def _(u):
                    prepare(u, far)
                    attend(u)
            else:
                u = b * heads_kv + first
                prepare(u, far)
                if u < first_early:
                    attend(u)
                elif u < units - 1:
                    e = u - first_early
                    attend_late(
                        heads_at_once, *group_refs(u), early.at[e], early_log.at[e], out_of(u)
                    )

    def wait_small_sends():
        for j in range(n):
            @pl.when(j != me)
            def _():
                pos_copy(me, j).wait_send()

        @pl.when(me == 0)
        def _():
            for d in range(1, nf):
                bias_copy(mf, lax.rem(mf + d, nf)).wait_send()
            for j in range(1, n):
                spread_copy(j).wait_send()

    def wait_end_sends():
        @pl.when(me == 0)
        def _():
            for p in range(len(ends)):
                to_right(me, ends, p).wait_send()

        @pl.when(me == n - 1)
        def _():
            for p in range(len(ends)):
                to_left(me, ends, p).wait_send()

    def wait_inner_sends():
        @pl.when(inner)
        def _():
            for j in range(n):
                pieces = ends if j in (0, n - 1) else middle
                for p in range(len(pieces)):
                    done = even & (p == marker)

                    @pl.when((j <= me) & ~(done & (far == 0) & (j == 1)))
                    def _():
                        to_right(j, pieces, p).wait_send()

                    @pl.when((j >= me) & ~(done & (far > 0) & (j == n - 2)))
                    def _():
                        to_left(j, pieces, p).wait_send()

    rotate_queries(0)
    pass_near(0)
    for b in range(1, batch):
        rotate_queries(b)
    for copy in own:
        copy.wait()
    for b in range(batch):
        prepare_entry(b, me)
    prepare_near(0)
    for b in range(1, batch - 1):
        if b == 1:
            hold_odd()
        pass_near(b)
        if b == 1:
            release_odd()
        prepare_near(b)
    @pl.when(~inner)
    def _():
        pass_near(batch - 1, [1])
        prepare_near(batch - 1, [1])

    wait_small_sends()
    wait_end_sends()
    for b in range(batch - 1):
        take_far(b)

    @pl.when(inner)
    def _():
        prepare_near(batch - 1)

    @pl.when(~inner)
    def _():
        pass_near(batch - 1, range(2, n))
        prepare_near(batch - 1, range(2, n))

    for e in range(early.shape[0]):
        attend_early(heads_at_once, *group_refs(first_early + e), early.at[e], early_log.at[e])
    take_far(batch - 1)
    wait_inner_sends()


def on_device(n, nf, q, k, v, bias, positions, rescale, table_index):
    batch, rows, width = q.shape
    heads_kv = k.shape[2] // HEAD_SIZE
    units = batch * heads_kv
    count = len(piece_list(batch, heads_kv, True))
    bias = bias.reshape(-1, HEAD_SIZE)
    hbm = pl.BlockSpec(memory_space=pltpu.HBM)
    dma = pltpu.SemaphoreType.DMA
    f32, bf16 = jnp.float32, jnp.bfloat16
    vmem = pl.BlockSpec(memory_space=pltpu.VMEM)
    heads_at_once = 8 if n <= 4 else 1
    early = jax.ShapeDtypeStruct((min(EARLY_GROUPS, heads_kv), GROUP * rows, HEAD_SIZE), f32)
    results = pl.pallas_call(
        functools.partial(kernel, n, nf, heads_at_once),
        out_shape=[
            jax.ShapeDtypeStruct(q.shape, bf16),
            jax.ShapeDtypeStruct((units, GROUP * rows, HEAD_SIZE), bf16),
            jax.ShapeDtypeStruct((units, n, rows, HEAD_SIZE), bf16),
            jax.ShapeDtypeStruct((units, n, rows, HEAD_SIZE), bf16),
            jax.ShapeDtypeStruct((batch, rows, n * rows), f32),
            early, early,
        ],
        in_specs=[hbm] * 7,
        out_specs=[vmem] * 7,
        scratch_shapes=[
            pltpu.SMEM(table_index.shape, jnp.int32),
            pltpu.VMEM((n,) + positions.shape, jnp.int32),
            pltpu.VMEM(rescale.shape, f32),
            dma((4,)),
            pltpu.VMEM((batch, rows, width), bf16),
            pltpu.VMEM((n, batch, 2) + k.shape[1:], bf16),
            pltpu.VMEM((batch, n, rows, HEAD_SIZE), f32),
            pltpu.VMEM((batch, n, rows, HEAD_SIZE), f32),
            pltpu.VMEM((nf,) + bias.shape, bf16),
            pltpu.VMEM((nf,) + bias.shape, f32),
            dma((batch,)), dma((2,)),
            dma((n, count)), dma((n, count)), dma((n, count)),
            dma((n,)), dma((n,)), dma((nf,)), dma((nf,)), dma((n,)), dma,
            pltpu.SemaphoreType.REGULAR((n,)), pltpu.SemaphoreType.REGULAR,
        ],
        compiler_params=pltpu.CompilerParams(
            collective_id=0, has_side_effects=True, vmem_limit_bytes=32 * 1024 * 1024
        ),
        name="relay_attention",
    )(*(pltpu.with_memory_space_constraint(x, pltpu.HBM) for x in (table_index, q, k, v, bias, positions, rescale)))
    return pl.pallas_call(
        functools.partial(write_kernel, heads_at_once),
        out_shape=jax.ShapeDtypeStruct(q.shape, bf16),
        in_specs=[vmem] * 7,
        out_specs=hbm,
        scratch_shapes=[pltpu.VMEM((rows, GROUP * HEAD_SIZE), bf16), dma((batch + 1,))],
        compiler_params=pltpu.CompilerParams(vmem_limit_bytes=24 * 1024 * 1024),
        name="write_result",
    )(*results)


def solution(mesh):
    in_specs = (
        P("fsdp", "ctx", "uly"),
        P("fsdp", "ctx", "uly"),
        P("fsdp", "ctx", "uly"),
        P("fsdp"),
        P("fsdp", "ctx"),
        P(),
        P("fsdp"),
    )
    n, nf = mesh.shape["ctx"], mesh.shape["fsdp"]
    return jax.shard_map(
        functools.partial(on_device, n, nf),
        mesh=mesh, in_specs=in_specs, out_specs=P("fsdp", "ctx", "uly"), check_vma=False,
    )
```

```python
import functools
import math

import jax
import jax.numpy as jnp
from jax import lax
from jax.experimental import pallas as pl
from jax.experimental.pallas import tpu as pltpu
from jax.sharding import PartitionSpec as P

QUERY_HEADS = 64
KEY_VALUE_HEADS = 8
HEAD_SIZE = 128
GROUP = QUERY_HEADS // KEY_VALUE_HEADS
RUN = 48
LATE_KEYS = 128
EARLY_GROUPS = 2

rope_base = 1000000.0
masked_value = -1e30
MESH = pl.DeviceIdType.MESH


def sine_cosine(angle):
    turns = jnp.floor(angle * (2.0 / math.pi) + 0.5)
    r = angle - turns * 1.5703125
    r = r - turns * 4.837512969970703125e-4
    r = r - turns * 7.54978995489188216e-8
    z = r * r
    s = r + r * z * (-1.6666654611e-1 + z * (8.3321608736e-3 - z * 1.9515295891e-4))
    c = 1.0 - 0.5 * z + z * z * (
        4.166664568298827e-2 + z * (-1.388731625493765e-3 + z * 2.443315711809948e-5)
    )
    quarter = turns.astype(jnp.int32) & 3
    odd = (quarter & 1) == 1
    sine = jnp.where(odd, c, s)
    cosine = jnp.where(odd, s, c)
    sine = jnp.where(quarter >= 2, -sine, sine)
    cosine = jnp.where((quarter == 1) | (quarter == 2), -cosine, cosine)
    return sine, cosine


def piece_list(batch, heads_kv, split_last):
    groups = [(b, 0, heads_kv) for b in range(batch)]
    if split_last:
        groups = groups[:-1] + [(batch - 1, g, 1) for g in range(heads_kv)]
    return groups


def group_scores(q_ref, k_ref, mask_ref, first, count, columns):
    shards, rows, _ = k_ref.shape
    s = lax.dot_general(
        q_ref[first * rows : (first + count) * rows, :],
        k_ref[...].reshape(shards * rows, HEAD_SIZE)[columns],
        (((1,), (1,)), ((), ())), preferred_element_type=jnp.float32,
    )
    wide = s.shape[1]
    s = s.reshape(count, rows, wide) + mask_ref[...][None, :, columns]
    return s.reshape(count * rows, wide)


def group_blend(p, v_ref, columns):
    shards, rows, _ = v_ref.shape
    return jnp.dot(
        p.astype(jnp.bfloat16), v_ref[...].reshape(shards * rows, HEAD_SIZE)[columns],
        preferred_element_type=jnp.float32,
    )


def store_heads(out_ref, o, first, count):
    rows = out_ref.shape[0]
    o = o.astype(jnp.bfloat16)
    for e in range(count):
        lanes = slice((first + e) * HEAD_SIZE, (first + e + 1) * HEAD_SIZE)
        out_ref[:, lanes] = o[e * rows : (e + 1) * rows]


SCALE = math.log2(math.e) / math.sqrt(HEAD_SIZE)


def attend_group(count, q_ref, k_ref, v_ref, mask_ref, out_ref):
    columns = slice(None)
    for i in range(0, GROUP, count):
        s = group_scores(q_ref, k_ref, mask_ref, i, count, columns)
        high = jnp.max(s, axis=-1, keepdims=True)
        p = jnp.exp2((s - high) * SCALE)
        total = jnp.sum(p, axis=-1, keepdims=True)
        store_heads(out_ref, group_blend(p, v_ref, columns) / total, i, count)


def attend_early(count, q_ref, k_ref, v_ref, mask_ref, part_ref, log_ref):
    rows = k_ref.shape[1]
    columns = slice(LATE_KEYS, None)
    for i in range(0, GROUP, count):
        at = slice(i * rows, (i + count) * rows)
        s = group_scores(q_ref, k_ref, mask_ref, i, count, columns)
        high = jnp.max(s, axis=-1, keepdims=True)
        p = jnp.exp2((s - high) * SCALE)
        total = jnp.sum(p, axis=-1, keepdims=True)
        part_ref[at, :] = group_blend(p, v_ref, columns) / total
        log_ref[at, :] = jnp.broadcast_to(
            high + jnp.log2(total) * (1.0 / SCALE), (count * rows, HEAD_SIZE)
        )


def attend_late(count, q_ref, k_ref, v_ref, mask_ref, part_ref, log_ref, out_ref):
    rows = k_ref.shape[1]
    columns = slice(0, LATE_KEYS)
    for i in range(0, GROUP, count):
        at = slice(i * rows, (i + count) * rows)
        s = group_scores(q_ref, k_ref, mask_ref, i, count, columns)
        before = log_ref[at, :]
        high = jnp.maximum(before, jnp.max(s, axis=-1, keepdims=True))
        p = jnp.exp2((s - high) * SCALE)
        keep = jnp.exp2((before - high) * SCALE)
        total = keep + jnp.sum(p, axis=-1, keepdims=True)
        o = (part_ref[at, :] * keep + group_blend(p, v_ref, columns)) / total
        store_heads(out_ref, o, i, count)


def write_kernel(
    heads_at_once, done_ref, q_ref, k_ref, v_ref, mask_ref, part_ref, log_ref,
    out_hbm, last, sems,
):
    batch = done_ref.shape[0]
    units, wide = q_ref.shape[0], last.shape[1]
    split = done_ref.shape[2] - wide
    copies = [
        pltpu.make_async_copy(done_ref.at[b], out_hbm.at[b], sems.at[b]) for b in range(batch - 1)
    ]
    if split:
        copies.append(pltpu.make_async_copy(
            done_ref.at[batch - 1, :, pl.ds(0, split)],
            out_hbm.at[batch - 1, :, pl.ds(0, split)], sems.at[batch - 1],
        ))
    for copy in copies:
        copy.start()
    u = units - 1
    e = part_ref.shape[0] - 1
    attend_late(
        heads_at_once, q_ref.at[u], k_ref.at[u], v_ref.at[u], mask_ref.at[batch - 1],
        part_ref.at[e], log_ref.at[e], last,
    )
    copy = pltpu.make_async_copy(
        last, out_hbm.at[batch - 1, :, pl.ds(split, wide)], sems.at[batch]
    )
    copy.start()
    for done in copies:
        done.wait()
    copy.wait()


def kernel(
    n, nf, heads_at_once,
    table_hbm, q_hbm, k_hbm, v_hbm, bias_hbm, pos_hbm, rescale_hbm,
    out_ref, q_rot, k_rot, v_all, mask_t, early, early_log,
    table_ref, pos_buf, rescale_ref, small_sem,
    q_buf, kv_buf, cos_t, sin_t, bias_buf, bias_f,
    q_sem, own_sem, send_right, send_left, recv_sem,
    pos_send, pos_recv, bias_send, bias_recv, spread_send, spread_recv, ready, turn,
):
    batch, rows, _ = q_hbm.shape
    heads_kv = k_hbm.shape[2] // HEAD_SIZE
    units = batch * heads_kv
    me = lax.axis_index("ctx")
    mf = lax.axis_index("fsdp")
    mu = lax.axis_index("uly")
    shard_rows = bias_hbm.shape[0]
    ends = piece_list(batch, heads_kv, True)
    middle = piece_list(batch, heads_kv, False)
    wide = GROUP * HEAD_SIZE
    far = jnp.where(2 * me <= n - 1, n - 1, 0)

    def slot_of(j):
        return jnp.where(far > 0, far - j, j)


    barrier = pltpu.get_barrier_semaphore()

    inner = (me > 0) & (me < n - 1)
    even = mf % 2 == 0

    @pl.when(inner & ~even)
    def _():
        pl.semaphore_signal(barrier, inc=1, device_id={"fsdp": mf - 1}, device_id_type=MESH)

    @pl.when(inner & even)
    def _():
        pl.semaphore_wait(barrier, 2)

    @pl.when((inner & ~even) | (me == n - 1))
    def _():
        pl.semaphore_wait(barrier, 1)

    @pl.when(me < n - 1)
    def _():
        pl.semaphore_signal(barrier, inc=1, device_id={"ctx": me + 1}, device_id_type=MESH)

    @pl.when(me == 0)
    def _():
        for d in range(1, nf):
            pl.semaphore_signal(
                barrier, inc=1, device_id={"fsdp": lax.rem(mf + d, nf)}, device_id_type=MESH
            )
        pl.semaphore_wait(barrier, nf - 1)

    def pos_copy(source, target):
        return pltpu.make_async_remote_copy(
            src_ref=pos_hbm, dst_ref=pos_buf.at[source],
            send_sem=pos_send.at[target], recv_sem=pos_recv.at[source],
            device_id={"ctx": target}, device_id_type=MESH,
        )

    def remote(shard, pieces, p, sems, target, source=None, kind=slice(None)):
        b, g, heads = pieces[p]
        lanes = pl.ds(g * HEAD_SIZE, heads * HEAD_SIZE)
        place = kv_buf.at[shard, b, kind, :, lanes]
        return pltpu.make_async_remote_copy(
            src_ref=place if source is None else source.at[b, :, lanes], dst_ref=place,
            send_sem=sems.at[shard, p], recv_sem=recv_sem.at[shard, p],
            device_id={"ctx": target}, device_id_type=MESH,
        )

    def to_right(shard, pieces, p, *own):
        return remote(shard, pieces, p, send_right, lax.rem(me + 1, n), *own)

    def to_left(shard, pieces, p, *own):
        return remote(shard, pieces, p, send_left, lax.rem(me + n - 1, n), *own)

    def start_own(to_side, pieces, first=0, last=None):
        for p in range(len(pieces))[first:last]:
            for kind, source in enumerate((k_hbm, v_hbm)):
                to_side(me, pieces, p, source, kind).start()

    def say_ready():
        for j in range(n - 2, -1, -1):
            @pl.when(j < me)
            def _():
                pl.semaphore_signal(
                    ready.at[me], inc=1, device_id={"ctx": j}, device_id_type=MESH
                )

        for j in range(n - 1):
            @pl.when(j < me)
            def _():
                pos_copy(me, j).start()

    @pl.when(me == n - 1)
    def _():
        say_ready()
        start_own(to_left, ends)

    @pl.when(inner)
    def _():
        start_own(to_left, middle, 0, 1)
        say_ready()

        @pl.when(me < n - 2)
        def _():
            start_own(to_left, middle, 1, None)

    small = [
        pltpu.make_async_copy(source, target, small_sem.at[i])
        for i, (source, target) in enumerate(
            (
                (pos_hbm, pos_buf.at[me]), (rescale_hbm, rescale_ref),
                (table_hbm, table_ref),
            )
        )
    ]
    own_bias = pltpu.make_async_copy(bias_hbm, bias_buf.at[mf], small_sem.at[3])
    for copy in small:
        copy.start()

    @pl.when(me == 0)
    def _():
        own_bias.start()

    def q_copy(b):
        return pltpu.make_async_copy(q_hbm.at[b], q_buf.at[b], q_sem.at[b])

    own = (
        pltpu.make_async_copy(k_hbm, kv_buf.at[me, :, 0], own_sem.at[0]),
        pltpu.make_async_copy(v_hbm, kv_buf.at[me, :, 1], own_sem.at[1]),
    )

    def bias_copy(source, target):
        return pltpu.make_async_remote_copy(
            src_ref=bias_hbm, dst_ref=bias_buf.at[source],
            send_sem=bias_send.at[target], recv_sem=bias_recv.at[source],
            device_id={"fsdp": target}, device_id_type=MESH,
        )

    def spread_copy(target):
        return pltpu.make_async_remote_copy(
            src_ref=bias_buf, dst_ref=bias_buf,
            send_sem=spread_send.at[target], recv_sem=spread_recv,
            device_id={"ctx": target}, device_id_type=MESH,
        )

    @pl.when(me == 0)
    def _():
        for d in range(1, nf):
            bias_copy(mf, lax.rem(mf + d, nf)).start()
        own_bias.wait()
        for d in range(1, nf):
            other = lax.rem(mf + d, nf)
            bias_copy(other, other).wait_recv()

    for j in range(1, n):
        @pl.when(me < j)
        def _():
            pl.semaphore_wait(ready.at[j], 1)

            if j == n - 1:
                @pl.when(me == n - 2)
                def _():
                    start_own(to_right, middle, 0, 1)

            pos_copy(me, j).start()

        @pl.when((me < j) & (me == 0))
        def _():
            spread_copy(j).start()

    @pl.when(me == 0)
    def _():
        start_own(to_right, ends)

    @pl.when(inner & (me < n - 2))
    def _():
        start_own(to_right, middle)

    @pl.when(me == n - 2)
    def _():
        start_own(to_right, middle, 1, None)
        start_own(to_left, middle, 1, None)

    for copy in own:
        copy.start()
    for b in range(batch):
        q_copy(b).start()
    for copy in small:
        copy.wait()

    @pl.when(me > 0)
    def _():
        spread_copy(0).wait_recv()

    for f in range(nf):
        bias_f[f] = bias_buf[f].astype(jnp.float32)

    def bias_row(row):
        return bias_f[row // shard_rows, pl.ds(row % shard_rows, 1), :]

    for j in range(n):
        @pl.when(j != me)
        def _():
            pos_copy(j, j).wait_recv()

    lane = lax.broadcasted_iota(jnp.int32, (1, HEAD_SIZE), 1)
    power = jnp.exp(
        (lane % (HEAD_SIZE // 2)).astype(jnp.float32)
        * (2.0 / HEAD_SIZE * math.log(rope_base))
    )
    low_half = lane < HEAD_SIZE // 2
    run_rows = lax.broadcasted_iota(jnp.int32, (RUN, HEAD_SIZE), 0)
    query_row = lax.broadcasted_iota(jnp.int32, (RUN, 1), 0)
    keys = n * rows
    key_lane = lax.broadcasted_iota(jnp.int32, (1, keys), 1)

    for b in range(batch):
        factors = rescale_ref[0:1, :]
        for t in range(1, rescale_ref.shape[0]):
            factors = jnp.where(table_ref[b] == t, rescale_ref[t : t + 1, :], factors)
        inverse = 1.0 / (jnp.concatenate([factors, factors], axis=1) * power)
        key_pos = key_lane % RUN
        for j in range(n):
            for piece in range(rows // RUN):
                first = pos_buf[j, b : b + 1, piece * RUN : piece * RUN + 1]
                here = key_lane // RUN == slot_of(j) * (rows // RUN) + piece
                key_pos = key_pos + jnp.where(here, first, 0)
                place = (run_rows + first).astype(jnp.float32)
                sine, cosine = sine_cosine(place * inverse)
                block = slice(piece * RUN, (piece + 1) * RUN)
                cos_t[b, j, block, :] = cosine
                sin_t[b, j, block, :] = jnp.where(low_half, -sine, sine)
        for piece in range(rows // RUN):
            first = pos_buf[me, b : b + 1, piece * RUN : piece * RUN + 1]
            mask_t[b, piece * RUN : (piece + 1) * RUN, :] = jnp.where(
                key_pos <= query_row + first, 0.0, masked_value
            )

    def rotate(x, cosine, sine):
        return x * cosine + pltpu.roll(x, HEAD_SIZE // 2, 1) * sine

    query_heads_here = heads_kv * GROUP

    def rotate_queries(b):
        q_copy(b).wait()

        @pl.loop(0, heads_kv)
        def _(g):
            for i in range(GROUP):
                x = q_buf[
                    b, :, pl.ds(pl.multiple_of(g * wide + i * HEAD_SIZE, HEAD_SIZE), HEAD_SIZE)
                ].astype(jnp.float32)
                x = x + bias_row(mu * query_heads_here + g * GROUP + i)
                q_rot[b * heads_kv + g, i * rows : (i + 1) * rows, :] = rotate(
                    x, cos_t[b, me], sin_t[b, me]
                ).astype(jnp.bfloat16)

    def prepare(u, j):
        b, g = u // heads_kv, u % heads_kv
        slot = slot_of(j)
        lanes = pl.ds(pl.multiple_of(g * HEAD_SIZE, HEAD_SIZE), HEAD_SIZE)
        x = kv_buf[j, b, 0, :, lanes].astype(jnp.float32)
        x = x + bias_row(QUERY_HEADS + mu * heads_kv + g)
        k_rot[u, slot] = rotate(x, cos_t[b, j], sin_t[b, j]).astype(jnp.bfloat16)
        x = kv_buf[j, b, 1, :, lanes].astype(jnp.float32)
        x = x + bias_row(QUERY_HEADS + KEY_VALUE_HEADS + mu * heads_kv + g)
        v_all[u, slot] = x.astype(jnp.bfloat16)

    def group_refs(u):
        return q_rot.at[u], k_rot.at[u], v_all.at[u], mask_t.at[u // heads_kv]

    def out_of(u):
        g = u % heads_kv
        return out_ref.at[u // heads_kv, :, pl.ds(pl.multiple_of(g * wide, wide), wide)]

    first_early = units - early.shape[0]

    def attend(u):
        attend_group(heads_at_once, *group_refs(u), out_of(u))

    def pass_left(shard, pieces, p):
        to_left(shard, pieces, p).wait_recv()

        @pl.when(me > 0)
        def _():
            to_left(shard, pieces, p).start()

    def pass_right(shard, pieces, p):
        to_right(shard, pieces, p).wait_recv()

        @pl.when(me < n - 1)
        def _():
            to_right(shard, pieces, p).start()

    def of_entry(pieces, b):
        return [p for p, piece in enumerate(pieces) if piece[0] == b]

    def prepare_entry(b, j):
        @pl.loop(b * heads_kv, (b + 1) * heads_kv)
        def _(u):
            prepare(u, j)

    def each_near(act, hops=range(1, n)):
        for hop in hops:
            right, left = me + hop, me - hop

            @pl.when((right < n) & (right != far))
            def _():
                act(right, pass_left, right == n - 1)

            @pl.when((left >= 0) & (left != far))
            def _():
                act(left, pass_right, left == 0)

    def pass_near(b, *hops):
        def act(shard, hand_on, at_end):
            for pieces, chosen in ((ends, at_end), (middle, ~at_end)):
                @pl.when(chosen)
                def _():
                    for p in of_entry(pieces, b):
                        hand_on(shard, pieces, p)

        each_near(act, *hops)

    def prepare_near(b, *hops):
        each_near(lambda shard, hand_on, at_end: prepare_entry(b, shard), *hops)

    def pass_far(p):
        to_left(far, ends, p).wait_recv()

        @pl.when(inner & (far > 0))
        def _():
            to_left(far, ends, p).start()

        @pl.when(inner & (far == 0))
        def _():
            to_right(far, ends, p).start()

    marker = of_entry(middle, 0)[-1]

    def hold_odd():
        @pl.when(inner & ~even)
        def _():
            pl.semaphore_wait(turn, 1)

    def release_odd():
        @pl.when(inner & even)
        def _():
            @pl.when(far > 0)
            def _():
                to_left(n - 2, middle, marker).wait_send()

            @pl.when(far == 0)
            def _():
                to_right(1, middle, marker).wait_send()

            pl.semaphore_signal(turn, inc=1, device_id={"fsdp": mf + 1}, device_id_type=MESH)

    def take_far(b):
        if b == batch - 1:
            @pl.when(inner)
            def _():
                for p in of_entry(ends, b):
                    pass_far(p)
        steps = {}
        for p in of_entry(ends, b):
            steps.setdefault(ends[p][1], []).append(p)
        starts = sorted(steps) + [heads_kv]
        for first, last in zip(starts, starts[1:]):
            for p in steps[first]:
                if b < batch - 1:
                    pass_far(p)
                else:
                    @pl.when(~inner)
                    def _():
                        to_left(far, ends, p).wait_recv()
            if b == batch - 2:
                @pl.when(inner)
                def _():
                    pass_near(batch - 1)
            if last - first > 1:
                @pl.loop(b * heads_kv + first, b * heads_kv + last)
                def _(u):
                    prepare(u, far)
                    attend(u)
            else:
                u = b * heads_kv + first
                prepare(u, far)
                if u < first_early:
                    attend(u)
                elif u < units - 1:
                    e = u - first_early
                    attend_late(
                        heads_at_once, *group_refs(u), early.at[e], early_log.at[e], out_of(u)
                    )

    def wait_small_sends():
        for j in range(n):
            @pl.when(j != me)
            def _():
                pos_copy(me, j).wait_send()

        @pl.when(me == 0)
        def _():
            for d in range(1, nf):
                bias_copy(mf, lax.rem(mf + d, nf)).wait_send()
            for j in range(1, n):
                spread_copy(j).wait_send()

    def wait_end_sends():
        @pl.when(me == 0)
        def _():
            for p in range(len(ends)):
                to_right(me, ends, p).wait_send()

        @pl.when(me == n - 1)
        def _():
            for p in range(len(ends)):
                to_left(me, ends, p).wait_send()

    def wait_inner_sends():
        @pl.when(inner)
        def _():
            for j in range(n):
                pieces = ends if j in (0, n - 1) else middle
                for p in range(len(pieces)):
                    done = even & (p == marker)

                    @pl.when((j <= me) & ~(done & (far == 0) & (j == 1)))
                    def _():
                        to_right(j, pieces, p).wait_send()

                    @pl.when((j >= me) & ~(done & (far > 0) & (j == n - 2)))
                    def _():
                        to_left(j, pieces, p).wait_send()

    rotate_queries(0)
    pass_near(0)
    for b in range(1, batch):
        rotate_queries(b)
    for copy in own:
        copy.wait()
    for b in range(batch):
        prepare_entry(b, me)
    prepare_near(0)
    for b in range(1, batch - 1):
        if b == 1:
            hold_odd()
        pass_near(b)
        if b == 1:
            release_odd()
        prepare_near(b)
    @pl.when(~inner)
    def _():
        pass_near(batch - 1, [1])
        prepare_near(batch - 1, [1])

    wait_small_sends()
    wait_end_sends()
    for b in range(batch - 1):
        take_far(b)

    @pl.when(inner)
    def _():
        prepare_near(batch - 1)

    @pl.when(~inner)
    def _():
        pass_near(batch - 1, range(2, n))
        prepare_near(batch - 1, range(2, n))

    for e in range(early.shape[0]):
        attend_early(heads_at_once, *group_refs(first_early + e), early.at[e], early_log.at[e])
    take_far(batch - 1)
    wait_inner_sends()


def on_device(n, nf, q, k, v, bias, positions, rescale, table_index):
    batch, rows, width = q.shape
    heads_kv = k.shape[2] // HEAD_SIZE
    units = batch * heads_kv
    count = len(piece_list(batch, heads_kv, True))
    bias = bias.reshape(-1, HEAD_SIZE)
    hbm = pl.BlockSpec(memory_space=pltpu.HBM)
    dma = pltpu.SemaphoreType.DMA
    f32, bf16 = jnp.float32, jnp.bfloat16
    vmem = pl.BlockSpec(memory_space=pltpu.VMEM)
    heads_at_once = 8 if n <= 4 else 1
    early = jax.ShapeDtypeStruct((min(EARLY_GROUPS, heads_kv), GROUP * rows, HEAD_SIZE), f32)
    results = pl.pallas_call(
        functools.partial(kernel, n, nf, heads_at_once),
        out_shape=[
            jax.ShapeDtypeStruct(q.shape, bf16),
            jax.ShapeDtypeStruct((units, GROUP * rows, HEAD_SIZE), bf16),
            jax.ShapeDtypeStruct((units, n, rows, HEAD_SIZE), bf16),
            jax.ShapeDtypeStruct((units, n, rows, HEAD_SIZE), bf16),
            jax.ShapeDtypeStruct((batch, rows, n * rows), f32),
            early, early,
        ],
        in_specs=[hbm] * 7,
        out_specs=[vmem] * 7,
        scratch_shapes=[
            pltpu.SMEM(table_index.shape, jnp.int32),
            pltpu.VMEM((n,) + positions.shape, jnp.int32),
            pltpu.VMEM(rescale.shape, f32),
            dma((4,)),
            pltpu.VMEM((batch, rows, width), bf16),
            pltpu.VMEM((n, batch, 2) + k.shape[1:], bf16),
            pltpu.VMEM((batch, n, rows, HEAD_SIZE), f32),
            pltpu.VMEM((batch, n, rows, HEAD_SIZE), f32),
            pltpu.VMEM((nf,) + bias.shape, bf16),
            pltpu.VMEM((nf,) + bias.shape, f32),
            dma((batch,)), dma((2,)),
            dma((n, count)), dma((n, count)), dma((n, count)),
            dma((n,)), dma((n,)), dma((nf,)), dma((nf,)), dma((n,)), dma,
            pltpu.SemaphoreType.REGULAR((n,)), pltpu.SemaphoreType.REGULAR,
        ],
        compiler_params=pltpu.CompilerParams(
            collective_id=0, has_side_effects=True, vmem_limit_bytes=32 * 1024 * 1024
        ),
        name="relay_attention",
    )(*(pltpu.with_memory_space_constraint(x, pltpu.HBM) for x in (table_index, q, k, v, bias, positions, rescale)))
    return pl.pallas_call(
        functools.partial(write_kernel, heads_at_once),
        out_shape=jax.ShapeDtypeStruct(q.shape, bf16),
        in_specs=[vmem] * 7,
        out_specs=hbm,
        scratch_shapes=[pltpu.VMEM((rows, GROUP * HEAD_SIZE), bf16), dma((batch + 1,))],
        compiler_params=pltpu.CompilerParams(vmem_limit_bytes=24 * 1024 * 1024),
        name="write_result",
    )(*results)


def solution(mesh):
    in_specs = (
        P("fsdp", "ctx", "uly"),
        P("fsdp", "ctx", "uly"),
        P("fsdp", "ctx", "uly"),
        P("fsdp"),
        P("fsdp", "ctx"),
        P(),
        P("fsdp"),
    )
    n, nf = mesh.shape["ctx"], mesh.shape["fsdp"]
    return jax.shard_map(
        functools.partial(on_device, n, nf),
        mesh=mesh, in_specs=in_specs, out_specs=P("fsdp", "ctx", "uly"), check_vma=False,
    )
```
